256 devices in a mesh: ctx: 256 (over x, z, y, core).
Axes of the slice: x: 4, y: 4, z: 8, core: 2. Of those that a mesh axis runs over, the one named last changes fastest.
Arguments:
- queries: bfloat16 [32768, 2048], P('ctx'), may hold values from -128 to 128
- key_heads: bfloat16 [32768, 512], P('ctx'), may hold values from -8 to 8
- value_heads: bfloat16 [32768, 512], P('ctx'), may hold values from -6 to 6
- out_grad: bfloat16 [32768, 2048], P('ctx'), may hold values from -6 to 6
- segment: int32 [32768], P('ctx'), may hold values from 0 to 63, never falling along the last dimension, each value on 1 to 2048 neighbouring positions
- sink_logits: float32 [32], replicated, may hold values from 0 to 4
Outputs:
- query_grad: bfloat16 [32768, 2048], P('ctx')
- key_grad: bfloat16 [32768, 512], P('ctx')
- value_grad: bfloat16 [32768, 512], P('ctx')
- sink_grad: float32 [32], replicated
The draws below stay inside these ranges and needn't reach their ends.
Inputs may be any that keep to these rules, and one draw needn't show every extreme that they name: `segment`: never falls along the tokens; each document holds 1 to 2048 tokens, one exactly that many.
All inputs are finite; a program needn't handle non-finite values.
Results may differ from the reference program's by a relative error of at most 0.008.
Values may be sent and summed in bfloat16 or wider, within the bound.
No kernel may reach another device: no remote copies, remote signals or barrier semaphores. Data moves between devices by JAX's collectives and lax.ppermute only.
A program may use at most 128 MiB of HBM per device.

```python
import math
import jax
import jax.numpy as jnp
import numpy as np
from jax import lax

QUERY_HEADS = 32
KV_HEADS = 8
HEAD_DIM = 64
WINDOW = 1024
TOK_DEV = 128
TOKENS = 32768


def shared_keys(key):
    base = jax.random.normal(jax.random.fold_in(key, 101), (TOKENS, KV_HEADS * HEAD_DIM), jnp.float32)
    base = jnp.clip(base, -5.0, 5.0)
    return base


def draw_key_heads(key, part):
    return shared_keys(key).astype(jnp.bfloat16)


def draw_queries(key, part):
    noise = jax.random.normal(jax.random.fold_in(key, 303), (TOKENS, QUERY_HEADS * HEAD_DIM), jnp.float32)
    noise = jnp.clip(noise, -5.0, 5.0)
    return noise.astype(jnp.bfloat16)


def shard_levels(own_key, shape, pieces, low, high):
    def one(dim, parts):
        steps = jax.random.uniform(jax.random.fold_in(jax.random.fold_in(own_key, 6), dim), (parts,), jnp.float32, low / len(pieces), high / len(pieces))
        return jnp.repeat(jnp.exp(steps), shape[dim] // parts).reshape((-1,) + (1,) * (len(shape) - dim - 1))

    gain = one(*pieces[0])
    for cut in pieces[1:]:
        gain = gain * one(*cut)
    return gain


def profile(number_of, total, bound, lean):
    loads = [(1 << 20) // math.isqrt(rank ** lean) + 1 for rank in range(2, number_of + 1)]
    surplus, counts = total - bound - (number_of - 1), [1] * (number_of - 1)
    while surplus > 0:
        movable = [i for i in range(number_of - 1) if counts[i] < bound]
        mass, remaining = sum([loads[i] for i in movable]), surplus
        for i in movable:
            extra = min(bound - counts[i], max(1, remaining * loads[i] // mass), surplus)
            counts[i] = counts[i] + extra
            surplus = surplus - extra
    return np.array([bound] + counts)


def uneven(stream_key, amount, total, limit, skew):
    if amount == 2:
        one = jax.random.randint(stream_key, (), max(1, total - limit), min(limit, total - 1) + 1)
        return jnp.stack([one, total - one])
    sizes = jnp.asarray(profile(amount, total, limit, skew), jnp.int32)
    pairs = (amount - 1) // 2
    source_of, taker = sizes[1:1 + 2 * pairs:2], sizes[2:2 + 2 * pairs:2]
    slack = jnp.minimum(source_of - 1, limit - taker)
    passed = jax.random.randint(jax.random.fold_in(stream_key, 1), (pairs,), 0, 1 << 20) % (slack + 1)
    sizes = sizes.at[1:1 + 2 * pairs:2].set(source_of - passed).at[2:2 + 2 * pairs:2].set(taker + passed)
    return sizes[jax.random.permutation(jax.random.fold_in(stream_key, 2), amount)]


def gaussian(own_key, shape, width, most, cuts=(), kind=jnp.bfloat16):
    drawn = width * jax.random.normal(own_key, shape, jnp.float32)
    if cuts:
        drawn = drawn * shard_levels(own_key, shape, cuts, -0.22, 0.18)
    return jnp.clip(drawn, -most, most).astype(kind)


def setup_inputs(seed: int = 0) -> dict:
    splits = jax.random.split(jax.random.key(seed), 7)
    queries = draw_queries(jax.random.fold_in(splits[6], 71), 0)
    key_heads = draw_key_heads(jax.random.fold_in(splits[6], 71), 0)
    value_heads = gaussian(splits[2], (TOKENS, KV_HEADS * HEAD_DIM), 1.0, 6.0, ((0, 256),))
    out_grad = gaussian(splits[3], (TOKENS, QUERY_HEADS * HEAD_DIM), 1.0, 6.0, ((0, 256),))
    segment = jnp.searchsorted(jnp.cumsum(uneven(splits[4], TOKENS // (4 * TOK_DEV), TOKENS, 16 * TOK_DEV, 2)), jnp.arange(TOKENS), side="right").astype(jnp.int32)
    sink_logits = jnp.clip(jax.random.uniform(splits[5], (QUERY_HEADS,), jnp.float32, 0.0, 4.0), 0.0, 4.0)
    return dict(queries=queries, key_heads=key_heads, value_heads=value_heads, out_grad=out_grad, segment=segment, sink_logits=sink_logits)


def block_grads(q_block, k_block, v_block, grad_block, allowed, sink_logits):
    groups = QUERY_HEADS // KV_HEADS
    score_scale = 1.0 / math.sqrt(HEAD_DIM)
    query_four = q_block.astype(jnp.float32).reshape(TOK_DEV, KV_HEADS, groups, HEAD_DIM)
    key_three = k_block.astype(jnp.float32).reshape(-1, KV_HEADS, HEAD_DIM)
    value_three = v_block.astype(jnp.float32).reshape(-1, KV_HEADS, HEAD_DIM)
    grad_four = grad_block.astype(jnp.float32).reshape(TOK_DEV, KV_HEADS, groups, HEAD_DIM)
    scores = jnp.einsum('bhgd,lhd->hgbl', query_four, key_three) * score_scale
    scores = jnp.where(allowed, scores, -jnp.inf)
    sink_grid = sink_logits.astype(jnp.float32).reshape(KV_HEADS, groups, 1, 1)
    top_value = jnp.maximum(lax.optimization_barrier(jnp.max(scores, -1, keepdims=True)), sink_grid)
    expd = jnp.exp(scores - top_value)
    sink_exp = jnp.exp(sink_grid - top_value)
    denom = lax.optimization_barrier(jnp.sum(expd, -1, keepdims=True)) + sink_exp
    probs = expd / denom
    sink_prob = (sink_exp / denom)[..., 0]
    weights = lax.optimization_barrier(probs.astype(jnp.bfloat16)).astype(jnp.float32)
    attended = jnp.einsum('hgbl,lhd->hgbd', weights, value_three)
    delta = jnp.einsum('bhgd,hgbd->hgb', grad_four, attended)
    dprob = jnp.einsum('bhgd,lhd->hgbl', grad_four, value_three)
    dscore = probs * (dprob - delta[..., None])
    dscore_b = lax.optimization_barrier(dscore.astype(jnp.bfloat16)).astype(jnp.float32)
    query_part = jnp.einsum('hgbl,lhd->bhgd', dscore_b, key_three) * score_scale
    key_part = jnp.einsum('hgbl,bhgd->lhd', dscore_b, query_four) * score_scale
    value_part = jnp.einsum('hgbl,bhgd->lhd', weights, grad_four)
    sink_part = -lax.optimization_barrier(jnp.sum(sink_prob * delta, -1)).reshape(QUERY_HEADS)
    query_part = query_part.reshape(TOK_DEV, QUERY_HEADS * HEAD_DIM).astype(jnp.bfloat16)
    key_part = key_part.reshape(-1, KV_HEADS * HEAD_DIM)
    value_part = value_part.reshape(-1, KV_HEADS * HEAD_DIM)
    return (query_part, key_part, value_part, sink_part)

def reference(queries, key_heads, value_heads, out_grad, segment, sink_logits):
    key_span = WINDOW + TOK_DEV
    kv_width = KV_HEADS * HEAD_DIM
    key_padded = jnp.concatenate([jnp.zeros((WINDOW, kv_width), key_heads.dtype), key_heads], 0)
    value_padded = jnp.concatenate([jnp.zeros((WINDOW, kv_width), value_heads.dtype), value_heads], 0)
    segment_padded = jnp.concatenate([jnp.full((WINDOW,), -1, jnp.int32), segment.astype(jnp.int32)], 0)
    query_pos = jnp.arange(TOK_DEV, dtype=jnp.int32)[:, None]
    key_pos = jnp.arange(key_span, dtype=jnp.int32)[None, :]
    inside = (key_pos > query_pos) & (key_pos <= query_pos + WINDOW)

    def one_block(running, block_index):
        key_acc, value_acc, sink_acc = running
        offset = (block_index * TOK_DEV).astype(jnp.int32)
        q_block = lax.dynamic_slice_in_dim(queries, offset, TOK_DEV, 0)
        grad_block = lax.dynamic_slice_in_dim(out_grad, offset, TOK_DEV, 0)
        k_block = lax.dynamic_slice_in_dim(key_padded, offset, key_span, 0)
        v_block = lax.dynamic_slice_in_dim(value_padded, offset, key_span, 0)
        seg_query = lax.dynamic_slice_in_dim(segment.astype(jnp.int32), offset, TOK_DEV, 0)
        seg_key = lax.dynamic_slice_in_dim(segment_padded, offset, key_span, 0)
        allowed = inside & (seg_query[:, None] == seg_key[None, :])
        query_part, key_part, value_part, sink_part = block_grads(q_block, k_block, v_block, grad_block, allowed, sink_logits)
        key_acc = lax.dynamic_update_slice_in_dim(key_acc, lax.dynamic_slice_in_dim(key_acc, offset, key_span, 0) + key_part, offset, 0)
        value_acc = lax.dynamic_update_slice_in_dim(value_acc, lax.dynamic_slice_in_dim(value_acc, offset, key_span, 0) + value_part, offset, 0)
        return ((key_acc, value_acc, sink_acc + sink_part), query_part)
    initial = (jnp.zeros((WINDOW + TOKENS, kv_width), jnp.float32), jnp.zeros((WINDOW + TOKENS, kv_width), jnp.float32), jnp.zeros((QUERY_HEADS,), jnp.float32))
    indices = jnp.arange(TOKENS // TOK_DEV, dtype=jnp.int32)
    (key_acc, value_acc, sink_acc), query_blocks = lax.scan(one_block, initial, indices)
    query_grad = query_blocks.reshape(TOKENS, QUERY_HEADS * HEAD_DIM)
    return (query_grad, key_acc[WINDOW:].astype(jnp.bfloat16), value_acc[WINDOW:].astype(jnp.bfloat16), sink_acc)
```

```python
import functools
import math

import jax
import jax.numpy as jnp
from jax import lax
from jax.experimental import pallas as pl
from jax.experimental.pallas import tpu as pltpu
from jax.sharding import PartitionSpec as P

KV_HEADS = 8
HEAD_DIM = 64
WINDOW = 1024
TOK = 128
CHIP = 2 * TOK
HOPS = WINDOW // CHIP
ROW = 4
SPAN = WINDOW + CHIP
HALF_KV = KV_HEADS // 2 * HEAD_DIM
SCALE = 1.0 / math.sqrt(HEAD_DIM)
EXP2_SCALE = SCALE * math.log2(math.e)
MASKED = -1e30
F32 = jnp.float32
BF16 = jnp.bfloat16


NT, NN = ((1,), (1,)), ((1,), (0,))


def dot(a, b, dims):
    return lax.dot_general(a, b, (dims, ((), ())), preferred_element_type=F32)


def mask_bias(place, chunk, own_chunk, hop):
    core, chip = place[0], place[1]
    key_seg = chunk[CHIP : CHIP + 16, :CHIP].astype(F32)[0:1]
    query_seg = own_chunk[CHIP : CHIP + 16, :CHIP].astype(F32)[0:1]
    key_seg = jnp.where(chip >= hop, key_seg, -1.0)
    column = jnp.transpose(jnp.broadcast_to(key_seg, (TOK, CHIP)))
    allowed = jnp.concatenate([column, column], 1) == query_seg
    if hop in (0, HOPS):
        query_pos = lax.broadcasted_iota(jnp.int32, (CHIP, CHIP), 1) ^ (core * TOK)
        key_pos = lax.broadcasted_iota(jnp.int32, (CHIP, CHIP), 0) ^ (core * TOK)
        inside = key_pos <= query_pos if hop == 0 else key_pos > query_pos
        allowed = allowed & inside
    return jnp.where(allowed, 0.0, MASKED)


def two_heads(place, own, peer, tile, p):
    at = tile * 512 + p * 128
    ours = own[:, pl.ds(pl.multiple_of(place[0] * 1024 + at, 128), 128)]
    theirs = peer[:, pl.ds(pl.multiple_of(at, 128), 128)]
    pair = jnp.concatenate([ours, theirs], 0).astype(F32)
    turned = pltpu.roll(pair, HEAD_DIM, 1)
    half = p // 2
    wanted = lax.broadcasted_iota(jnp.int32, (CHIP, 128), 1) // HEAD_DIM == half
    return [
        jnp.where(wanted, pair if half == e else turned, 0.0).astype(BF16) for e in range(2)
    ]


def lane_tile(tile, first_lane=0):
    return pl.ds(pl.multiple_of(first_lane + tile * 128, 128), 128)


def stats_kernel(
    hop, last, place, sinks, q_own, q_peer, g_own, g_peer, chunk, own_chunk, *refs
):
    before, after, bias = refs[:3], refs[3:-1], refs[-1]
    if hop == 0:
        before, after = None, refs[:-1]
    core = place[0]
    bias[...] = mask_bias(place, chunk, own_chunk, hop)

    def of_tile(tile, carry):
        key_tile = chunk[0:CHIP, lane_tile(tile)]
        value_tile = chunk[0:CHIP, lane_tile(tile, HALF_KV)]
        for p in range(4):
            query = two_heads(place, q_own, q_peer, tile, p)
            grad = two_heads(place, g_own, g_peer, tile, p)
            for e in range(2):
                head = tile * 8 + 2 * p + e
                at = pl.ds(head, 1)
                sink = sinks[core * 16 + head] * (1.0 / SCALE)
                s = dot(key_tile, query[e], NT) + bias[...]
                dp = dot(value_tile, grad[e], NT)
                old = jnp.full((1, CHIP), sink, F32) if hop == 0 else before[0][at, :]
                top = jnp.maximum(old, jnp.max(s, 0, keepdims=True))
                ex = jnp.exp2((s - top) * EXP2_SCALE)
                fade = jnp.exp2((old - top) * EXP2_SCALE)
                denom = jnp.sum(ex, 0, keepdims=True)
                weighed = jnp.sum(ex * dp, 0, keepdims=True)
                if hop == 0:
                    denom = denom + fade
                else:
                    denom = denom + before[1][at, :] * fade
                    weighed = weighed + before[2][at, :] * fade
                after[0][at, :] = top
                if last:
                    share = 1.0 / denom
                    delta = weighed * share
                    after[1][at, :] = share
                    after[2][at, :] = delta
                    after[3][at, :] = -jnp.exp2((sink - top) * EXP2_SCALE) * share * delta
                else:
                    after[1][at, :] = denom
                    after[2][at, :] = weighed
        return carry

    lax.fori_loop(0, 2, of_tile, 0)


def parts_kernel(
    hop, tiles, place, q_own, q_peer, g_own, g_peer, chunk, own_chunk, tops, shares, deltas, *refs
):
    bias, keys_t, weight, dscore, query_all, grad_all = refs[-6:]
    dq_in = None if hop == HOPS else refs[0]
    outs = refs[:-6] if hop == HOPS else refs[1:-6]
    kv_out = outs[0]
    base, width = tiles[0], 128 * len(tiles)
    bias[...] = mask_bias(place, chunk, own_chunk, hop)
    keys_t[...] = jnp.transpose(chunk[0:CHIP, 0:CHIP].astype(F32)).astype(BF16)

    def of_tile(tile, carry):
        key_tile = chunk[0:CHIP, lane_tile(tile)]
        value_tile = chunk[0:CHIP, lane_tile(tile, HALF_KV)]
        for p in range(4):
            query = two_heads(place, q_own, q_peer, tile, p)
            grad = two_heads(place, g_own, g_peer, tile, p)
            for e in range(2):
                at = pl.ds(tile * 8 + 2 * p + e, 1)
                span = slice((2 * p + e) * CHIP, (2 * p + e + 1) * CHIP)
                query_all[span, :] = query[e]
                grad_all[span, :] = grad[e]
                s = dot(key_tile, query[e], NT) + bias[...]
                dp = dot(value_tile, grad[e], NT)
                prob = jnp.exp2((s - tops[at, :]) * EXP2_SCALE) * shares[at, :]
                weight[:, span] = prob.astype(BF16)
                dscore[:, span] = (prob * (dp - deltas[at, :])).astype(BF16)
        value_part = dot(weight[...], grad_all[...], NN)
        key_part = dot(dscore[...], query_all[...], NN) * SCALE
        kv_out[:, lane_tile(tile - base)] = key_part.astype(kv_out.dtype)
        kv_out[:, lane_tile(tile - base, width)] = value_part.astype(kv_out.dtype)
        for group in range(2):
            key_rows = pl.ds(
                pl.multiple_of((2 * tile + group) * HEAD_DIM, HEAD_DIM), HEAD_DIM
            )
            g = 2 * (tile - base) + group
            rows = pl.ds(pl.multiple_of(g * HEAD_DIM, HEAD_DIM), HEAD_DIM)
            dq_t = dot(keys_t[key_rows, :], dscore[:, group * 1024 : (group + 1) * 1024], NN)
            if dq_in is not None:
                dq_t = dq_t + dq_in[rows, :]
            if hop > 0:
                outs[1][rows, :] = dq_t
            else:
                for pair in range(2):
                    two = jnp.concatenate(
                        [
                            dq_t[:, (2 * pair + e) * CHIP : (2 * pair + e + 1) * CHIP]
                            for e in range(2)
                        ],
                        0,
                    )
                    dq = (jnp.transpose(two) * SCALE).astype(BF16)
                    lanes = lane_tile(2 * g + pair)
                    outs[1][:, lanes] = dq[:TOK]
                    outs[2][:, lanes] = dq[TOK:]
        return carry

    if len(tiles) == 2:
        lax.fori_loop(0, 2, of_tile, 0)
    else:
        of_tile(base, 0)


def pack_kernel(place, keys, values, segment, queries, grads, own, send, tokens):
    core = place[0]

    def half(ref, which, width):
        return ref[:, pl.ds(pl.multiple_of(which * width, width), width)]

    marks = jnp.broadcast_to(segment[...], (16, TOK)).astype(F32).astype(BF16)
    for out, which in ((own, core), (send, 1 - core)):
        out[:TOK, :HALF_KV] = half(keys, which, HALF_KV)
        out[:TOK, HALF_KV:] = half(values, which, HALF_KV)
        for lane in range(0, 2 * HALF_KV, TOK):
            out[TOK:, lane : lane + TOK] = marks
    tokens[:TOK, :] = half(queries, 1 - core, 1024)
    tokens[TOK:, :] = half(grads, 1 - core, 1024)


def join_kernel(place, mine, theirs, *outs):
    core = place[0]
    width = mine.shape[1] // len(outs)
    for n, out in enumerate(outs):
        for which, part in ((core, mine), (1 - core, theirs)):
            at = pl.ds(pl.multiple_of(which * width, width), width)
            out[:, at] = part[:, n * width : (n + 1) * width]


SMEM = pl.BlockSpec(memory_space=pltpu.SMEM)
VMEM = pl.BlockSpec(memory_space=pltpu.VMEM)
STAT = jax.ShapeDtypeStruct((16, CHIP), F32)


def run(kernel, name, n_scalars, operands, out_shape, scratch, flops, interpret):
    n_arrays = len(operands) - n_scalars
    return pl.pallas_call(
        kernel,
        name=name,
        in_specs=[SMEM] * n_scalars + [VMEM] * n_arrays,
        out_specs=[VMEM] * len(out_shape),
        out_shape=out_shape,
        scratch_shapes=scratch,
        compiler_params=pltpu.CompilerParams(vmem_limit_bytes=32 << 20),
        cost_estimate=pl.CostEstimate(flops=flops, transcendentals=0, bytes_accessed=1 << 20),
        interpret=interpret,
    )(*operands)


def stats_of(hop, last, place, sinks, tokens, chunk, own_chunk, before, interpret):
    return run(
        functools.partial(stats_kernel, hop, last), f"stats_{hop}", 2,
        (place, sinks, *tokens, chunk, own_chunk, *before),
        [STAT] * (4 if last else 3),
        [pltpu.VMEM((CHIP, CHIP), F32)], 2 << 30, interpret,
    )


def parts_of(hop, tiles, place, tokens, chunk, own_chunk, stats, dq, interpret):
    width = 128 * len(tiles)
    kv = jax.ShapeDtypeStruct((CHIP, 2 * width), BF16 if hop else F32)
    if hop:
        dq_shapes = [jax.ShapeDtypeStruct((width, 1024), F32)]
    else:
        dq_shapes = [jax.ShapeDtypeStruct((TOK, 4 * width), BF16)] * 2
    return run(
        functools.partial(parts_kernel, hop, tiles), f"parts_{hop}_{tiles[0]}", 1,
        (place, *tokens, chunk, own_chunk, *stats, *dq),
        [kv] + dq_shapes,
        [
            pltpu.VMEM((CHIP, CHIP), F32),
            pltpu.VMEM((CHIP, CHIP), BF16),
            pltpu.VMEM((CHIP, 8 * CHIP), BF16),
            pltpu.VMEM((CHIP, 8 * CHIP), BF16),
            pltpu.VMEM((8 * CHIP, 128), BF16),
            pltpu.VMEM((8 * CHIP, 128), BF16),
        ],
        3 << 30, interpret,
    )


def packed(place, key_heads, value_heads, segment, queries, out_grad, interpret):
    rows = jax.ShapeDtypeStruct((TOK + 16, 2 * HALF_KV), BF16)
    return run(
        pack_kernel, "pack", 1,
        (place, key_heads, value_heads, segment[None, :], queries, out_grad),
        [rows, rows, jax.ShapeDtypeStruct((2 * TOK, 1024), BF16)], [], 1 << 20, interpret,
    )


def joined(place, mine, theirs, outs, interpret):
    width = mine.shape[1] // outs
    shape = jax.ShapeDtypeStruct((TOK, 2 * width), BF16)
    return run(
        join_kernel, "join", 1, (place, mine, theirs), [shape] * outs, [], 1 << 20, interpret
    )


def per_device(count, interpret, queries, key_heads, value_heads, out_grad, segment, sink_logits):
    index = lax.axis_index("ctx")
    core, chip = index % 2, index // 2
    first = core == 0

    def sent(block, route):
        return lax.ppermute(block, "ctx", route)

    def shifted(block, chips):
        return sent(block, [(i, (i + 2 * chips) % count) for i in range(count)])

    def crossed(block, bit):
        return lax.ppermute(block, "ctx", [(i, i ^ bit) for i in range(count)])

    def in_row(i, hop):
        return i // 8 * 8 + (i // 2 + hop) % ROW * 2 + i % 2

    place = jnp.stack([core, chip]).astype(jnp.int32)
    own, kv_send, tokens_send = packed(
        place, key_heads, value_heads, segment, queries, out_grad, interpret
    )
    came = crossed(kv_send, 1)
    marks = jnp.concatenate(
        [own[TOK:, :TOK], came[TOK:, TOK:CHIP], own[TOK:, CHIP:]], 1
    )
    chunk = jnp.concatenate([own[:TOK], came[:TOK], marks], 0)
    chunks = {0: chunk, HOPS: shifted(chunk, HOPS)}
    both = crossed(tokens_send, 1)
    tokens = (queries, both[:TOK], out_grad, both[TOK:])
    stats = stats_of(
        0, False, place, sink_logits, tokens, chunk, chunk, (), interpret
    )
    *stats, chunks[HOPS] = lax.optimization_barrier((*stats, chunks[HOPS]))
    for hop in range(1, HOPS):
        within = chip % ROW + hop < ROW
        chunks[hop] = sent(
            jnp.where(within, chunk, chunks[HOPS]), [(i, in_row(i, hop)) for i in range(count)]
        )
    for hop in (HOPS, 1, 2, 3):
        stats = stats_of(
            hop, hop == 3, place, sink_logits, tokens, chunks[hop], chunk, stats, interpret
        )
    sink_half = jnp.sum(stats[3], -1)
    zeros = jnp.zeros_like(sink_half)
    sink_grad = jnp.where(
        first, jnp.concatenate([sink_half, zeros]), jnp.concatenate([zeros, sink_half])
    )
    bits = [1 << n for n in range(count.bit_length() - 1)]

    def widened(value):
        return value + crossed(value, bits.pop(0)) if bits else value

    *stats, sink_grad = lax.optimization_barrier((*stats[:3], widened(sink_grad)))
    dq, came_back, totals, dq_parts = {}, {}, [], []
    tile_sets = {4: ((0, 1),), 3: ((0, 1),), 2: ((0, 1),), 1: ((0,), (1,)), 0: ((0,), (1,))}
    for hop in range(HOPS, -1, -1):
        pieces = []
        for tiles in tile_sets[hop]:
            if len(tiles) == 1 and len(dq) == 1:
                whole = dq[(0, 1)]
                dq = {(0,): whole[:128], (1,): whole[128:]}
            before = [dq[tiles]] if tiles in dq else []
            piece, *after = parts_of(
                hop, tiles, place, tokens, chunks[hop], chunk, stats, before, interpret
            )
            pieces.append(piece)
            if hop == 0:
                dq_parts.append(after)
                if tiles == (0,):
                    sink_grad, dq[(1,)] = lax.optimization_barrier(
                        (widened(sink_grad), dq[(1,)])
                    )
                continue
            dq[tiles] = after[0]
            if tiles == tile_sets[hop][-1]:
                if len(pieces) == 2:
                    piece = jnp.concatenate(
                        [x[:, :128] for x in pieces] + [x[:, 128:] for x in pieces], 1
                    )
                came_back[hop] = shifted(piece, -hop)
            sink_grad = widened(sink_grad)
            tied = [n for n in came_back if n == hop + 1]
            keys = list(dq)
            flat = lax.optimization_barrier(
                (sink_grad, *[dq[n] for n in keys], *[came_back[n] for n in tied])
            )
            sink_grad = flat[0]
            dq = dict(zip(keys, flat[1:]))
            came_back.update(zip(tied, flat[1 + len(keys) :]))
        if hop == 0:
            totals = pieces
    dq_own = jnp.concatenate([x[0] for x in dq_parts], 1)
    dq_peer = jnp.concatenate([x[1] for x in dq_parts], 1)
    (query_grad,) = joined(place, dq_own, crossed(dq_peer, 1), 1, interpret)
    total = jnp.concatenate([x[:, :128] for x in totals] + [x[:, 128:] for x in totals], 1)
    for part in came_back.values():
        total = total + part.astype(F32)
    total = total.astype(BF16)
    key_grad, value_grad = joined(place, total[:TOK], crossed(total[TOK:], 1), 2, interpret)
    while bits:
        sink_grad = widened(sink_grad)
    return query_grad, key_grad, value_grad, sink_grad


def solution(mesh, interpret=False):
    rows = P("ctx", None)
    return jax.shard_map(
        functools.partial(per_device, mesh.size, interpret),
        mesh=mesh,
        in_specs=(rows, rows, rows, rows, P("ctx"), P()),
        out_specs=(rows, rows, rows, P()),
        check_vma=False,
    )
```

```python
import functools
import math

import jax
import jax.numpy as jnp
from jax import lax
from jax.experimental import pallas as pl
from jax.experimental.pallas import tpu as pltpu
from jax.sharding import PartitionSpec as P

KV_HEADS = 8
HEAD_DIM = 64
WINDOW = 1024
TOK = 128
CHIP = 2 * TOK
HOPS = WINDOW // CHIP
ROW = 4
SPAN = WINDOW + CHIP
HALF_KV = KV_HEADS // 2 * HEAD_DIM
SCALE = 1.0 / math.sqrt(HEAD_DIM)
EXP2_SCALE = SCALE * math.log2(math.e)
MASKED = -1e30
F32 = jnp.float32
BF16 = jnp.bfloat16


NT, NN = ((1,), (1,)), ((1,), (0,))


def dot(a, b, dims):
    return lax.dot_general(a, b, (dims, ((), ())), preferred_element_type=F32)


def mask_bias(place, chunk, own_chunk, hop):
    core, chip = place[0], place[1]
    key_seg = chunk[CHIP : CHIP + 16, :CHIP].astype(F32)[0:1]
    query_seg = own_chunk[CHIP : CHIP + 16, :CHIP].astype(F32)[0:1]
    key_seg = jnp.where(chip >= hop, key_seg, -1.0)
    column = jnp.transpose(jnp.broadcast_to(key_seg, (TOK, CHIP)))
    allowed = jnp.concatenate([column, column], 1) == query_seg
    if hop in (0, HOPS):
        query_pos = lax.broadcasted_iota(jnp.int32, (CHIP, CHIP), 1) ^ (core * TOK)
        key_pos = lax.broadcasted_iota(jnp.int32, (CHIP, CHIP), 0) ^ (core * TOK)
        inside = key_pos <= query_pos if hop == 0 else key_pos > query_pos
        allowed = allowed & inside
    return jnp.where(allowed, 0.0, MASKED)


def prep_kernel(place, q_own, g_own, both_peer, query_all, grad_all):
    core = place[0]
    q_peer, g_peer = both_peer.at[:TOK, :], both_peer.at[TOK:, :]
    lane_half = lax.broadcasted_iota(jnp.int32, (CHIP, 128), 1) // HEAD_DIM
    for own, peer, out in ((q_own, q_peer, query_all), (g_own, g_peer, grad_all)):
        for pair in range(8):
            at = pl.ds(pl.multiple_of(core * 1024 + pair * 128, 128), 128)
            theirs = peer[:, pair * 128 : (pair + 1) * 128]
            rows = jnp.concatenate([own[:, at], theirs], 0).astype(F32)
            turned = pltpu.roll(rows, HEAD_DIM, 1)
            half = pair // 2 % 2
            for e in range(2):
                chosen = jnp.where(lane_half == half, rows if half == e else turned, 0.0)
                out[head_rows(2 * pair + e), :] = chosen.astype(BF16)


def head_rows(head):
    return slice(head * CHIP, (head + 1) * CHIP)


def lane_tile(tile, first_lane=0):
    return slice(first_lane + tile * 128, first_lane + tile * 128 + 128)


def stats_kernel(hop, last, place, sinks, query_all, grad_all, chunk, own_chunk, *refs):
    before, after = refs[:3], refs[3:]
    if hop == 0:
        before, after = None, refs
    (top_out, second, third), bias = after[:3], after[-1]
    core = place[0]
    bias[...] = mask_bias(place, chunk, own_chunk, hop)
    for head in range(16):
        tile, at = head // 8, slice(head, head + 1)
        sink = sinks[core * 16 + head] * (1.0 / SCALE)
        s = dot(chunk[0:CHIP, lane_tile(tile)], query_all[head_rows(head), :], NT) + bias[...]
        dp = dot(chunk[0:CHIP, lane_tile(tile, HALF_KV)], grad_all[head_rows(head), :], NT)
        old = jnp.full((1, CHIP), sink, F32) if hop == 0 else before[0][at, :]
        top = jnp.maximum(old, jnp.max(s, 0, keepdims=True))
        ex = jnp.exp2((s - top) * EXP2_SCALE)
        fade = jnp.exp2((old - top) * EXP2_SCALE)
        denom = jnp.sum(ex, 0, keepdims=True)
        weighed = jnp.sum(ex * dp, 0, keepdims=True)
        if hop == 0:
            denom = denom + fade
        else:
            denom = denom + before[1][at, :] * fade
            weighed = weighed + before[2][at, :] * fade
        top_out[at, :] = top
        if last:
            share = 1.0 / denom
            delta = weighed * share
            second[at, :] = share
            third[at, :] = delta
            after[3][at, :] = -jnp.exp2((sink - top) * EXP2_SCALE) * share * delta
        else:
            second[at, :] = denom
            third[at, :] = weighed


def parts_kernel(
    hop, place, query_all, grad_all, chunk, own_chunk, tops, shares, deltas, *refs
):
    weight, dscore, bias = refs[-3:]
    dq_in = None if hop == HOPS else refs[0]
    outs = refs[:-3] if hop == HOPS else refs[1:-3]
    kv_out = outs[0]
    bias[...] = mask_bias(place, chunk, own_chunk, hop)
    keys_t = jnp.transpose(chunk[0:CHIP, 0:CHIP].astype(F32)).astype(BF16)
    for tile in range(2):
        for n in range(8):
            head, span = 8 * tile + n, head_rows(n)
            at = slice(head, head + 1)
            s = dot(chunk[0:CHIP, lane_tile(tile)], query_all[head_rows(head), :], NT)
            dp = dot(
                chunk[0:CHIP, lane_tile(tile, HALF_KV)], grad_all[head_rows(head), :], NT
            )
            prob = jnp.exp2((s + bias[...] - tops[at, :]) * EXP2_SCALE) * shares[at, :]
            weight[tile, :, span] = prob.astype(BF16)
            dscore[tile, :, span] = (prob * (dp - deltas[at, :])).astype(BF16)
        rows = slice(8 * tile * CHIP, 8 * (tile + 1) * CHIP)
        value_part = dot(weight[tile], grad_all[rows, :], NN)
        key_part = dot(dscore[tile], query_all[rows, :], NN) * SCALE
        kv_out[:, lane_tile(tile)] = key_part.astype(kv_out.dtype)
        kv_out[:, lane_tile(tile, HALF_KV)] = value_part.astype(kv_out.dtype)
        for group in range(2):
            g = 2 * tile + group
            rows = slice(g * HEAD_DIM, (g + 1) * HEAD_DIM)
            dq_t = dot(
                keys_t[rows, :], dscore[tile, :, group * 1024 : (group + 1) * 1024], NN
            )
            if dq_in is not None:
                dq_t = dq_t + dq_in[rows, :]
            if hop > 0:
                outs[1][rows, :] = dq_t
                continue
            for pair in range(2):
                two = jnp.concatenate(
                    [dq_t[:, head_rows(2 * pair)], dq_t[:, head_rows(2 * pair + 1)]], 0
                )
                dq = (jnp.transpose(two) * SCALE).astype(BF16)
                outs[1][:, lane_tile(2 * g + pair)] = dq[:TOK]
                outs[2][:, lane_tile(2 * g + pair)] = dq[TOK:]


def pack_kernel(place, segment, keys, values, queries, grads, own, send, tokens, sems):
    core = place[0]

    def half(ref, which, width):
        return ref.at[:, pl.ds(pl.multiple_of(which * width, width), width)]

    moves = []
    for out, which in ((send, 1 - core), (own, core)):
        moves.append((half(keys, which, HALF_KV), out.at[:TOK, :HALF_KV]))
        moves.append((half(values, which, HALF_KV), out.at[:TOK, HALF_KV:]))
    moves.append((half(queries, 1 - core, 1024), tokens.at[:TOK, :]))
    moves.append((half(grads, 1 - core, 1024), tokens.at[TOK:, :]))
    copies = [
        pltpu.make_async_copy(source, target, sems.at[n])
        for n, (source, target) in enumerate(moves)
    ]
    for copy in copies:
        copy.start()
    marks = jnp.broadcast_to(segment[...], (16, TOK)).astype(F32).astype(BF16)
    for out in (own, send):
        for lane in range(0, 2 * HALF_KV, TOK):
            out[TOK:, lane : lane + TOK] = marks
    for copy in copies:
        copy.wait()


def join_kernel(place, mine, theirs, *outs):
    core = place[0]
    width = mine.shape[1] // len(outs)
    for n, out in enumerate(outs):
        for which, part in ((core, mine), (1 - core, theirs)):
            at = pl.ds(pl.multiple_of(which * width, width), width)
            out[:, at] = part[:, n * width : (n + 1) * width]


SMEM = pl.BlockSpec(memory_space=pltpu.SMEM)
VMEM = pl.BlockSpec(memory_space=pltpu.VMEM)
STAT = jax.ShapeDtypeStruct((16, CHIP), F32)


def run(
    kernel, name, n_scalars, operands, out_shape, scratch, flops, interpret, n_far=0, vmem=16
):
    n_arrays = len(operands) - n_scalars - n_far
    return pl.pallas_call(
        kernel,
        name=name,
        in_specs=[SMEM] * n_scalars
        + [VMEM] * n_arrays
        + [pl.BlockSpec(memory_space=pltpu.HBM)] * n_far,
        out_specs=[VMEM] * len(out_shape),
        out_shape=out_shape,
        scratch_shapes=scratch,
        compiler_params=pltpu.CompilerParams(vmem_limit_bytes=vmem << 20),
        cost_estimate=pl.CostEstimate(flops=flops, transcendentals=0, bytes_accessed=1 << 20),
        interpret=interpret,
    )(*operands)


def prepared(place, queries, out_grad, both_peer, interpret):
    rows = jax.ShapeDtypeStruct((16 * CHIP, 128), BF16)
    return run(
        prep_kernel, "prep", 1, (place, queries, out_grad, both_peer),
        [rows, rows], [], 1 << 30, interpret,
    )


def stats_of(hop, last, place, sinks, tokens, chunk, own_chunk, before, interpret):
    return run(
        functools.partial(stats_kernel, hop, last), f"stats_{hop}", 2,
        (place, sinks, *tokens, chunk, own_chunk, *before),
        [STAT] * (4 if last else 3),
        [pltpu.VMEM((CHIP, CHIP), F32)], 2 << 30, interpret,
    )


def parts_of(hop, place, tokens, chunk, own_chunk, stats, dq, interpret):
    kv = jax.ShapeDtypeStruct((CHIP, 2 * HALF_KV), BF16 if hop else F32)
    if hop:
        dq_shapes = [jax.ShapeDtypeStruct((CHIP, 1024), F32)]
    else:
        dq_shapes = [jax.ShapeDtypeStruct((TOK, 1024), BF16)] * 2
    return run(
        functools.partial(parts_kernel, hop), f"parts_{hop}", 1,
        (place, *tokens, chunk, own_chunk, *stats, *dq),
        [kv] + dq_shapes,
        [pltpu.VMEM((2, CHIP, 8 * CHIP), BF16)] * 2 + [pltpu.VMEM((CHIP, CHIP), F32)],
        3 << 30, interpret,
    )


def packed(place, key_heads, value_heads, segment, queries, out_grad, interpret):
    rows = jax.ShapeDtypeStruct((TOK + 16, 2 * HALF_KV), BF16)
    return run(
        pack_kernel, "pack", 1,
        (place, segment[None, :], key_heads, value_heads, queries, out_grad),
        [rows, rows, jax.ShapeDtypeStruct((2 * TOK, 1024), BF16)],
        [pltpu.SemaphoreType.DMA((6,))], 1 << 20, interpret, n_far=4, vmem=62,
    )


def joined(place, mine, theirs, outs, interpret):
    width = mine.shape[1] // outs
    shape = jax.ShapeDtypeStruct((TOK, 2 * width), BF16)
    return run(
        join_kernel, "join", 1, (place, mine, theirs), [shape] * outs, [], 1 << 20, interpret
    )


def per_device(count, interpret, queries, key_heads, value_heads, out_grad, segment, sink_logits):
    index = lax.axis_index("ctx")
    core, chip = index % 2, index // 2
    first = core == 0

    def sent(block, route):
        return lax.ppermute(block, "ctx", route)

    def shifted(block, chips):
        return sent(block, [(i, (i + 2 * chips) % count) for i in range(count)])

    def crossed(block, bit):
        return lax.ppermute(block, "ctx", [(i, i ^ bit) for i in range(count)])

    def in_row(i, hop):
        return i // 8 * 8 + (i // 2 + hop) % ROW * 2 + i % 2

    place = jnp.stack([core, chip]).astype(jnp.int32)
    own, kv_send, tokens_send = packed(
        place, key_heads, value_heads, segment, queries, out_grad, interpret
    )
    came, tokens_send = lax.optimization_barrier((crossed(kv_send, 1), tokens_send))
    marks = jnp.concatenate(
        [own[TOK:, :TOK], came[TOK:, TOK:CHIP], own[TOK:, CHIP:]], 1
    )
    chunk = jnp.concatenate([own[:TOK], came[:TOK], marks], 0)
    chunks = {0: chunk, HOPS: shifted(chunk, HOPS)}
    both = crossed(tokens_send, 1)
    tokens = prepared(place, queries, out_grad, both, interpret)
    stats = stats_of(
        0, False, place, sink_logits, tokens, chunk, chunk, (), interpret
    )
    *stats, chunks[HOPS] = lax.optimization_barrier((*stats, chunks[HOPS]))
    for hop in range(1, HOPS):
        within = chip % ROW + hop < ROW
        chunks[hop] = sent(
            jnp.where(within, chunk, chunks[HOPS]), [(i, in_row(i, hop)) for i in range(count)]
        )
    for hop in (HOPS, 1, 2, 3):
        stats = stats_of(
            hop, hop == 3, place, sink_logits, tokens, chunks[hop], chunk, stats, interpret
        )
    *stats, sink_rows = stats
    sink_grad = jnp.sum(sink_rows, -1)
    bits = [1 << n for n in range(1, count.bit_length() - 1)]

    def widened(value):
        return value + crossed(value, bits.pop(0)) if bits else value

    dq, came_back = (), {}
    for hop in range(HOPS, 0, -1):
        part, *dq = parts_of(hop, place, tokens, chunks[hop], chunk, stats, dq, interpret)
        came_back[hop] = shifted(part, -hop)
        sink_grad = widened(sink_grad)
        if hop + 1 in came_back:
            dq[0], sink_grad, came_back[hop + 1] = lax.optimization_barrier(
                (dq[0], sink_grad, came_back[hop + 1])
            )
        else:
            dq[0], sink_grad = lax.optimization_barrier((dq[0], sink_grad))
    total, dq_own, dq_peer = parts_of(0, place, tokens, chunk, chunk, stats, dq, interpret)
    dq_own, dq_peer, sink_grad = lax.optimization_barrier(
        (dq_own, dq_peer, widened(sink_grad))
    )
    dq_came = crossed(dq_peer, 1)
    query_grad = jnp.where(
        first,
        jnp.concatenate([dq_own, dq_came], 1),
        jnp.concatenate([dq_came, dq_own], 1),
    )
    for part in came_back.values():
        total = total + part.astype(F32)
    total = total.astype(BF16)
    key_grad, value_grad = joined(place, total[:TOK], crossed(total[TOK:], 1), 2, interpret)
    while bits:
        sink_grad = widened(sink_grad)
    other = crossed(sink_grad, 1)
    sink_grad = jnp.where(
        first, jnp.concatenate([sink_grad, other]), jnp.concatenate([other, sink_grad])
    )
    return query_grad, key_grad, value_grad, sink_grad


def solution(mesh, interpret=False):
    rows = P("ctx", None)
    return jax.shard_map(
        functools.partial(per_device, mesh.size, interpret),
        mesh=mesh,
        in_specs=(rows, rows, rows, rows, P("ctx"), P()),
        out_specs=(rows, rows, rows, P()),
        check_vma=False,
    )
```

```python
import functools
import math

import jax
import jax.numpy as jnp
from jax import lax
from jax.experimental import pallas as pl
from jax.experimental.pallas import tpu as pltpu
from jax.sharding import PartitionSpec as P

KV_HEADS = 8
HEAD_DIM = 64
WINDOW = 1024
TOK = 128
CHIP = 2 * TOK
HOPS = WINDOW // CHIP
ROW = 4
SPAN = WINDOW + CHIP
HALF_KV = KV_HEADS // 2 * HEAD_DIM
SCALE = 1.0 / math.sqrt(HEAD_DIM)
EXP2_SCALE = SCALE * math.log2(math.e)
MASKED = -1e30
F32 = jnp.float32
BF16 = jnp.bfloat16


NT, NN = ((1,), (1,)), ((1,), (0,))


def dot(a, b, dims):
    return lax.dot_general(a, b, (dims, ((), ())), preferred_element_type=F32)


def mask_bias(place, chunk, own_chunk, hop):
    core, chip = place[0], place[1]
    key_seg = chunk[CHIP : CHIP + 16, :CHIP].astype(F32)[0:1]
    query_seg = own_chunk[CHIP : CHIP + 16, :CHIP].astype(F32)[0:1]
    key_seg = jnp.where(chip >= hop, key_seg, -1.0)
    column = jnp.transpose(jnp.broadcast_to(key_seg, (TOK, CHIP)))
    allowed = jnp.concatenate([column, column], 1) == query_seg
    if hop in (0, HOPS):
        query_pos = lax.broadcasted_iota(jnp.int32, (CHIP, CHIP), 1) ^ (core * TOK)
        key_pos = lax.broadcasted_iota(jnp.int32, (CHIP, CHIP), 0) ^ (core * TOK)
        inside = key_pos <= query_pos if hop == 0 else key_pos > query_pos
        allowed = allowed & inside
    return jnp.where(allowed, 0.0, MASKED)


def prep_kernel(place, q_own, g_own, both_peer, rows_all):
    query_all, grad_all = split_rows(rows_all)
    core = place[0]
    q_peer, g_peer = both_peer.at[:TOK, :], both_peer.at[TOK:, :]
    lane_half = lax.broadcasted_iota(jnp.int32, (CHIP, 128), 1) // HEAD_DIM
    for own, peer, out in ((q_own, q_peer, query_all), (g_own, g_peer, grad_all)):
        for pair in range(8):
            at = pl.ds(pl.multiple_of(core * 1024 + pair * 128, 128), 128)
            theirs = peer[:, pair * 128 : (pair + 1) * 128]
            rows = jnp.concatenate([own[:, at], theirs], 0).astype(F32)
            turned = pltpu.roll(rows, HEAD_DIM, 1)
            half = pair // 2 % 2
            for e in range(2):
                chosen = jnp.where(lane_half == half, rows if half == e else turned, 0.0)
                out[head_rows(2 * pair + e), :] = chosen.astype(BF16)


def split_rows(rows_all):
    return rows_all.at[: 16 * CHIP, :], rows_all.at[16 * CHIP :, :]


def head_rows(head):
    return slice(head * CHIP, (head + 1) * CHIP)


def lane_tile(tile, first_lane=0):
    return slice(first_lane + tile * 128, first_lane + tile * 128 + 128)


def stats_kernel(hop, last, place, sinks, rows_all, chunk, own_chunk, *refs):
    query_all, grad_all = split_rows(rows_all)
    before, after = refs[:3], refs[3:]
    if hop == 0:
        before, after = None, refs
    top_out, second, third = after[:3]
    bias, sink_rows = after[-2:]
    core = place[0]
    bias[...] = mask_bias(place, chunk, own_chunk, hop)
    for head in range(16):
        tile, at = head // 8, slice(head, head + 1)
        sink = sinks[core * 16 + head] * (1.0 / SCALE)
        s = dot(chunk[0:CHIP, lane_tile(tile)], query_all[head_rows(head), :], NT) + bias[...]
        dp = dot(chunk[0:CHIP, lane_tile(tile, HALF_KV)], grad_all[head_rows(head), :], NT)
        old = jnp.full((1, CHIP), sink, F32) if hop == 0 else before[0][at, :]
        top = jnp.maximum(old, jnp.max(s, 0, keepdims=True))
        ex = jnp.exp2((s - top) * EXP2_SCALE)
        fade = jnp.exp2((old - top) * EXP2_SCALE)
        denom = jnp.sum(ex, 0, keepdims=True)
        weighed = jnp.sum(ex * dp, 0, keepdims=True)
        if hop == 0:
            denom = denom + fade
        else:
            denom = denom + before[1][at, :] * fade
            weighed = weighed + before[2][at, :] * fade
        top_out[at, :] = top
        if last:
            share = 1.0 / denom
            delta = weighed * share
            second[at, :] = share
            third[at, :] = delta
            sink_rows[at, :] = -jnp.exp2((sink - top) * EXP2_SCALE) * share * delta
        else:
            second[at, :] = denom
            third[at, :] = weighed
    if last:
        sums = jnp.sum(sink_rows[...], 1, keepdims=True)
        after[3][...] = jnp.transpose(jnp.broadcast_to(sums, (16, 128)))[0:1, :]


def parts_kernel(
    hop, place, rows_all, chunk, own_chunk, tops, shares, deltas, *refs
):
    query_all, grad_all = split_rows(rows_all)
    weight, dscore, bias = refs[-3:]
    dq_in = None if hop == HOPS else refs[0]
    outs = refs[:-3] if hop == HOPS else refs[1:-3]
    kv_out = outs[0]
    bias[...] = mask_bias(place, chunk, own_chunk, hop)
    keys_t = jnp.transpose(chunk[0:CHIP, 0:CHIP].astype(F32)).astype(BF16)
    for tile in range(2):
        for n in range(8):
            head, span = 8 * tile + n, head_rows(n)
            at = slice(head, head + 1)
            s = dot(chunk[0:CHIP, lane_tile(tile)], query_all[head_rows(head), :], NT)
            dp = dot(
                chunk[0:CHIP, lane_tile(tile, HALF_KV)], grad_all[head_rows(head), :], NT
            )
            prob = jnp.exp2((s + bias[...] - tops[at, :]) * EXP2_SCALE) * shares[at, :]
            weight[tile, :, span] = prob.astype(BF16)
            dscore[tile, :, span] = (prob * (dp - deltas[at, :])).astype(BF16)
        rows = slice(8 * tile * CHIP, 8 * (tile + 1) * CHIP)
        value_part = dot(weight[tile], grad_all[rows, :], NN)
        key_part = dot(dscore[tile], query_all[rows, :], NN) * SCALE
        kv_out[:, lane_tile(tile)] = key_part.astype(kv_out.dtype)
        kv_out[:, lane_tile(tile, HALF_KV)] = value_part.astype(kv_out.dtype)
        for group in range(2):
            g = 2 * tile + group
            rows = slice(g * HEAD_DIM, (g + 1) * HEAD_DIM)
            dq_t = dot(
                keys_t[rows, :], dscore[tile, :, group * 1024 : (group + 1) * 1024], NN
            )
            if dq_in is not None:
                dq_t = dq_t + dq_in[rows, :]
            if hop > 0:
                outs[1][rows, :] = dq_t
                continue
            for pair in range(2):
                two = jnp.concatenate(
                    [dq_t[:, head_rows(2 * pair)], dq_t[:, head_rows(2 * pair + 1)]], 0
                )
                dq = (jnp.transpose(two) * SCALE).astype(BF16)
                outs[1][:, lane_tile(2 * g + pair)] = dq[:TOK]
                outs[2][:, lane_tile(2 * g + pair)] = dq[TOK:]


SMEM = pl.BlockSpec(memory_space=pltpu.SMEM)
VMEM = pl.BlockSpec(memory_space=pltpu.VMEM)
STAT = jax.ShapeDtypeStruct((16, CHIP), F32)


def run(kernel, name, n_scalars, operands, out_shape, scratch, flops, interpret):
    n_arrays = len(operands) - n_scalars
    return pl.pallas_call(
        kernel,
        name=name,
        in_specs=[SMEM] * n_scalars + [VMEM] * n_arrays,
        out_specs=[VMEM] * len(out_shape),
        out_shape=out_shape,
        scratch_shapes=scratch,
        compiler_params=pltpu.CompilerParams(vmem_limit_bytes=16 << 20),
        cost_estimate=pl.CostEstimate(flops=flops, transcendentals=0, bytes_accessed=1 << 20),
        interpret=interpret,
    )(*operands)


def prepared(place, queries, out_grad, both_peer, interpret):
    rows = jax.ShapeDtypeStruct((32 * CHIP, 128), BF16)
    return run(
        prep_kernel, "prep", 1, (place, queries, out_grad, both_peer),
        [rows], [], 1 << 30, interpret,
    )


def stats_of(hop, last, place, sinks, tokens, chunk, own_chunk, before, interpret):
    return run(
        functools.partial(stats_kernel, hop, last), f"stats_{hop}", 2,
        (place, sinks, *tokens, chunk, own_chunk, *before),
        [STAT] * 3 + [jax.ShapeDtypeStruct((1, 16), F32)] * last,
        [pltpu.VMEM((CHIP, CHIP), F32), pltpu.VMEM((16, CHIP), F32)], 2 << 30, interpret,
    )


def parts_of(hop, place, tokens, chunk, own_chunk, stats, dq, interpret):
    kv = jax.ShapeDtypeStruct((CHIP, 2 * HALF_KV), BF16 if hop else F32)
    if hop:
        dq_shapes = [jax.ShapeDtypeStruct((CHIP, 1024), F32)]
    else:
        dq_shapes = [jax.ShapeDtypeStruct((TOK, 1024), BF16)] * 2
    return run(
        functools.partial(parts_kernel, hop), f"parts_{hop}", 1,
        (place, *tokens, chunk, own_chunk, *stats, *dq),
        [kv] + dq_shapes,
        [pltpu.VMEM((2, CHIP, 8 * CHIP), BF16)] * 2 + [pltpu.VMEM((CHIP, CHIP), F32)],
        3 << 30, interpret,
    )


def per_device(count, interpret, queries, key_heads, value_heads, out_grad, segment, sink_logits):
    index = lax.axis_index("ctx")
    core, chip = index % 2, index // 2
    first = core == 0

    def sent(block, route):
        return lax.ppermute(block, "ctx", route)

    def shifted(block, chips):
        return sent(block, [(i, (i + 2 * chips) % count) for i in range(count)])

    def crossed(block, bit):
        return lax.ppermute(block, "ctx", [(i, i ^ bit) for i in range(count)])

    def in_row(i, hop):
        return i // 8 * 8 + (i // 2 + hop) % ROW * 2 + i % 2

    place = jnp.stack([core, chip]).astype(jnp.int32)
    def either(array, middle):
        return array[:, :middle], array[:, middle:]

    k_low, k_high = either(key_heads, HALF_KV)
    v_low, v_high = either(value_heads, HALF_KV)
    kv_low = jnp.concatenate([k_low, v_low], 1)
    kv_high = jnp.concatenate([k_high, v_high], 1)
    own, send = jnp.where(first, kv_low, kv_high), jnp.where(first, kv_high, kv_low)
    marks = jnp.pad(segment.astype(BF16)[None, :], ((0, 15), (0, 2 * HALF_KV - TOK)))
    kv_send = jnp.concatenate([send, marks], 0)
    queries, out_grad, kv_send = lax.optimization_barrier((queries, out_grad, kv_send))
    q_low, q_high = either(queries, 1024)
    g_low, g_high = either(out_grad, 1024)
    tokens_send = jnp.concatenate(
        [jnp.where(first, q_high, q_low), jnp.where(first, g_high, g_low)], 0
    )
    came, tokens_send = lax.optimization_barrier((crossed(kv_send, 1), tokens_send))
    marks_both = jnp.concatenate([marks[:, :TOK], came[TOK:, :TOK], marks[:, CHIP:]], 1)
    chunk = jnp.concatenate([own, came[:TOK], marks_both], 0)
    chunks = {0: chunk, HOPS: shifted(chunk, HOPS)}
    both = crossed(tokens_send, 1)
    tokens = prepared(place, queries, out_grad, both, interpret)
    stats = stats_of(
        0, False, place, sink_logits, tokens, chunk, chunk, (), interpret
    )
    *stats, chunks[HOPS] = lax.optimization_barrier((*stats, chunks[HOPS]))
    for hop in range(1, HOPS):
        within = chip % ROW + hop < ROW
        chunks[hop] = sent(
            jnp.where(within, chunk, chunks[HOPS]), [(i, in_row(i, hop)) for i in range(count)]
        )
    for hop in (HOPS, 1, 2, 3):
        stats = stats_of(
            hop, hop == 3, place, sink_logits, tokens, chunks[hop], chunk, stats, interpret
        )
    *stats, sink_row = stats
    sink_grad = sink_row.reshape(16)
    bits = [bit for bit in (4, 16, 32, 128, 8, 64, 2) if bit < count]

    def widened(value):
        return value + crossed(value, bits.pop(0)) if bits else value

    dq, came_back = (), {}
    for hop in range(HOPS, 0, -1):
        part, *dq = parts_of(hop, place, tokens, chunks[hop], chunk, stats, dq, interpret)
        part, sink_grad = lax.optimization_barrier((part, widened(sink_grad)))
        came_back[hop] = shifted(part, -hop)
        if hop > 1:
            sink_grad = widened(sink_grad)
        else:
            sink_half, sink_grad = sink_grad, crossed(sink_grad, 1)
        if hop < HOPS:
            dq[0], sink_grad, came_back[hop + 1] = lax.optimization_barrier(
                (dq[0], sink_grad, came_back[hop + 1])
            )
        else:
            dq[0], sink_grad = lax.optimization_barrier((dq[0], sink_grad))
    total, dq_own, dq_peer = parts_of(0, place, tokens, chunk, chunk, stats, dq, interpret)

    def joined(mine, theirs):
        return jnp.where(
            first, jnp.concatenate([mine, theirs], 1), jnp.concatenate([theirs, mine], 1)
        )

    sink_grad = jnp.where(
        first,
        jnp.concatenate([sink_half, sink_grad]),
        jnp.concatenate([sink_grad, sink_half]),
    )
    query_grad = joined(dq_own, crossed(dq_peer, 1))
    for part in came_back.values():
        total = total + part.astype(F32)
    total = total.astype(BF16)
    came, query_grad = lax.optimization_barrier((crossed(total[TOK:], 1), query_grad))
    key_grad = joined(total[:TOK, :HALF_KV], came[:, :HALF_KV])
    value_grad = joined(total[:TOK, HALF_KV:], came[:, HALF_KV:])
    return query_grad, key_grad, value_grad, sink_grad


def solution(mesh, interpret=False):
    rows = P("ctx", None)
    return jax.shard_map(
        functools.partial(per_device, mesh.size, interpret),
        mesh=mesh,
        in_specs=(rows, rows, rows, rows, P("ctx"), P()),
        out_specs=(rows, rows, rows, P()),
        check_vma=False,
    )
```

```python
import functools
import math

import jax
import jax.numpy as jnp
from jax import lax
from jax.experimental import pallas as pl
from jax.experimental.pallas import tpu as pltpu
from jax.sharding import Mesh
from jax.sharding import PartitionSpec as P

KV_HEADS = 8
HEAD_DIM = 64
WINDOW = 1024
TOK = 128
CHIP = 2 * TOK
HOPS = WINDOW // CHIP
ROW = 4
SINK_ROWS = 256
AXES = ("far", "y", "core")
SPAN = WINDOW + CHIP
HALF_KV = KV_HEADS // 2 * HEAD_DIM
SCALE = 1.0 / math.sqrt(HEAD_DIM)
EXP2_SCALE = SCALE * math.log2(math.e)
MASKED = -1e30
F32 = jnp.float32
BF16 = jnp.bfloat16


NT, NN = ((1,), (1,)), ((1,), (0,))


def dot(a, b, dims):
    return lax.dot_general(a, b, (dims, ((), ())), preferred_element_type=F32)


def mask_bias(place, chunk, own_chunk, hop):
    core, chip = place[0], place[1]
    key_seg = chunk[CHIP : CHIP + 16, :CHIP].astype(F32)[0:1]
    query_seg = own_chunk[CHIP : CHIP + 16, :CHIP].astype(F32)[0:1]
    key_seg = jnp.where(chip >= hop, key_seg, -1.0)
    column = jnp.transpose(jnp.broadcast_to(key_seg, (TOK, CHIP)))
    allowed = jnp.concatenate([column, column], 1) == query_seg
    if hop in (0, HOPS):
        query_pos = lax.broadcasted_iota(jnp.int32, (CHIP, CHIP), 1) ^ (core * TOK)
        key_pos = lax.broadcasted_iota(jnp.int32, (CHIP, CHIP), 0) ^ (core * TOK)
        inside = key_pos <= query_pos if hop == 0 else key_pos > query_pos
        allowed = allowed & inside
    return jnp.where(allowed, 0.0, MASKED)


def prep_kernel(place, q_own, g_own, both_peer, rows_all):
    query_all, grad_all = split_rows(rows_all)
    core = place[0]
    q_peer, g_peer = both_peer.at[:TOK, :], both_peer.at[TOK:, :]
    lane_half = lax.broadcasted_iota(jnp.int32, (CHIP, 128), 1) // HEAD_DIM
    for own, peer, out in ((q_own, q_peer, query_all), (g_own, g_peer, grad_all)):
        for pair in range(8):
            at = pl.ds(pl.multiple_of(core * 1024 + pair * 128, 128), 128)
            theirs = peer[:, pair * 128 : (pair + 1) * 128]
            rows = jnp.concatenate([own[:, at], theirs], 0).astype(F32)
            turned = pltpu.roll(rows, HEAD_DIM, 1)
            half = pair // 2 % 2
            for e in range(2):
                chosen = jnp.where(lane_half == half, rows if half == e else turned, 0.0)
                out[head_rows(2 * pair + e), :] = chosen.astype(BF16)


def split_rows(rows_all):
    return rows_all.at[: 16 * CHIP, :], rows_all.at[16 * CHIP :, :]


def head_rows(head):
    return slice(head * CHIP, (head + 1) * CHIP)


def lane_tile(tile, first_lane=0):
    return slice(first_lane + tile * 128, first_lane + tile * 128 + 128)


def stats_kernel(hop, last, place, sinks, rows_all, chunk, own_chunk, *refs):
    query_all, grad_all = split_rows(rows_all)
    before, after = refs[:3], refs[3:]
    if hop == 0:
        before, after = None, refs
    top_out, second, third = after[:3]
    bias, sink_rows = after[-2:]
    core = place[0]
    bias[...] = mask_bias(place, chunk, own_chunk, hop)
    def of_tile(tile, carry):
        lanes = pl.ds(pl.multiple_of(tile * 128, 128), 128)
        value_lanes = pl.ds(pl.multiple_of(HALF_KV + tile * 128, 128), 128)
        for n in range(8):
            head = tile * 8 + n
            at, rows = pl.ds(head, 1), pl.ds(pl.multiple_of(head * CHIP, CHIP), CHIP)
            sink = sinks[core * 16 + head] * (1.0 / SCALE)
            s = dot(chunk[0:CHIP, lanes], query_all[rows, :], NT) + bias[...]
            dp = dot(chunk[0:CHIP, value_lanes], grad_all[rows, :], NT)
            old = jnp.full((1, CHIP), sink, F32) if hop == 0 else before[0][at, :]
            top = jnp.maximum(old, jnp.max(s, 0, keepdims=True))
            ex = jnp.exp2((s - top) * EXP2_SCALE)
            fade = jnp.exp2((old - top) * EXP2_SCALE)
            denom = jnp.sum(ex, 0, keepdims=True)
            weighed = jnp.sum(ex * dp, 0, keepdims=True)
            if hop == 0:
                denom = denom + fade
            else:
                denom = denom + before[1][at, :] * fade
                weighed = weighed + before[2][at, :] * fade
            top_out[at, :] = top
            if last:
                share = 1.0 / denom
                delta = weighed * share
                second[at, :] = share
                third[at, :] = delta
                sink_rows[at, :] = -jnp.exp2((sink - top) * EXP2_SCALE) * share * delta
            else:
                second[at, :] = denom
                third[at, :] = weighed
        return carry

    lax.fori_loop(0, 2, of_tile, 0)
    if last:
        sums = jnp.sum(sink_rows[...], 1, keepdims=True)
        for row in range(0, SINK_ROWS, 16):
            after[3][row : row + 16, :] = jnp.broadcast_to(sums, (16, 128))


def parts_kernel(
    hop, place, rows_all, chunk, own_chunk, tops, shares, deltas, *refs
):
    query_all, grad_all = split_rows(rows_all)
    weight, dscore, bias, keys_t = refs[-4:]
    dq_in = None if hop == HOPS else refs[0]
    outs = refs[:-4] if hop == HOPS else refs[1:-4]
    kv_out = outs[0]
    bias[...] = mask_bias(place, chunk, own_chunk, hop)
    keys_t[...] = jnp.transpose(chunk[0:CHIP, 0:CHIP].astype(F32)).astype(BF16)

    def part(start, size, unit):
        return pl.ds(pl.multiple_of(start * unit, unit), size * unit)

    def of_tile(tile, carry):
        lanes, value_lanes = part(tile, 1, 128), part(tile + HALF_KV // 128, 1, 128)
        for n in range(8):
            span, rows = head_rows(n), part(8 * tile + n, 1, CHIP)
            at = pl.ds(8 * tile + n, 1)
            s = dot(chunk[0:CHIP, lanes], query_all[rows, :], NT)
            dp = dot(chunk[0:CHIP, value_lanes], grad_all[rows, :], NT)
            prob = jnp.exp2((s + bias[...] - tops[at, :]) * EXP2_SCALE) * shares[at, :]
            weight[:, span] = prob.astype(BF16)
            dscore[:, span] = (prob * (dp - deltas[at, :])).astype(BF16)
        rows = part(tile, 1, 8 * CHIP)
        value_part = dot(weight[...], grad_all[rows, :], NN)
        key_part = dot(dscore[...], query_all[rows, :], NN) * SCALE
        kv_out[:, lanes] = key_part.astype(kv_out.dtype)
        kv_out[:, value_lanes] = value_part.astype(kv_out.dtype)
        for group in range(2):
            rows = part(2 * tile + group, 1, HEAD_DIM)
            dq_t = dot(keys_t[rows, :], dscore[:, group * 1024 : (group + 1) * 1024], NN)
            if dq_in is not None:
                dq_t = dq_t + dq_in[rows, :]
            if hop > 0:
                outs[1][rows, :] = dq_t
                continue
            for pair in range(2):
                two = jnp.concatenate(
                    [dq_t[:, head_rows(2 * pair)], dq_t[:, head_rows(2 * pair + 1)]], 0
                )
                dq = (jnp.transpose(two) * SCALE).astype(BF16)
                at = part(4 * tile + 2 * group + pair, 1, 128)
                outs[1][:, at] = dq[:TOK]
                outs[2][:, at] = dq[TOK:]
        return carry

    if hop in (1, 2):
        lax.fori_loop(0, 2, of_tile, 0)
    else:
        of_tile(1, of_tile(0, 0))


def fold_kernel(gathered, out):
    total = gathered[0:2]
    for n in range(1, ROW):
        total = total + gathered[2 * n : 2 * n + 2]
    out[...] = jnp.concatenate(
        [jnp.transpose(total[0])[0:1, :], jnp.transpose(total[1])[0:1, :]], 1
    )


def folded(gathered, interpret):
    return pl.pallas_call(
        fold_kernel,
        name="fold",
        grid=(1,),
        in_specs=[pl.BlockSpec((2 * ROW, 16, 128), lambda i: (0, 0, 0))],
        out_specs=pl.BlockSpec((1, 32), lambda i: (0, 0)),
        out_shape=jax.ShapeDtypeStruct((1, 32), F32),
        interpret=interpret,
    )(gathered).reshape(32)


SMEM = pl.BlockSpec(memory_space=pltpu.SMEM)
VMEM = pl.BlockSpec(memory_space=pltpu.VMEM)
STAT = jax.ShapeDtypeStruct((16, CHIP), F32)


def run(kernel, name, n_scalars, operands, out_shape, scratch, flops, interpret):
    n_arrays = len(operands) - n_scalars
    return pl.pallas_call(
        kernel,
        name=name,
        in_specs=[SMEM] * n_scalars + [VMEM] * n_arrays,
        out_specs=[VMEM] * len(out_shape),
        out_shape=out_shape,
        scratch_shapes=scratch,
        compiler_params=pltpu.CompilerParams(vmem_limit_bytes=16 << 20),
        cost_estimate=pl.CostEstimate(flops=flops, transcendentals=0, bytes_accessed=1 << 20),
        interpret=interpret,
    )(*operands)


def prepared(place, queries, out_grad, both_peer, interpret):
    rows = jax.ShapeDtypeStruct((32 * CHIP, 128), BF16)
    return run(
        prep_kernel, "prep", 1, (place, queries, out_grad, both_peer),
        [rows], [], 1 << 30, interpret,
    )


def stats_of(hop, last, place, sinks, tokens, chunk, own_chunk, before, interpret):
    return run(
        functools.partial(stats_kernel, hop, last), f"stats_{hop}", 2,
        (place, sinks, *tokens, chunk, own_chunk, *before),
        [STAT] * 3 + [jax.ShapeDtypeStruct((SINK_ROWS, 128), F32)] * last,
        [pltpu.VMEM((CHIP, CHIP), F32), pltpu.VMEM((16, CHIP), F32)], 2 << 30, interpret,
    )


def parts_of(hop, place, tokens, chunk, own_chunk, stats, dq, interpret):
    kv = jax.ShapeDtypeStruct((CHIP, 2 * HALF_KV), BF16 if hop else F32)
    if hop:
        dq_shapes = [jax.ShapeDtypeStruct((CHIP, 1024), F32)]
    else:
        dq_shapes = [jax.ShapeDtypeStruct((TOK, 1024), BF16)] * 2
    return run(
        functools.partial(parts_kernel, hop), f"parts_{hop}", 1,
        (place, *tokens, chunk, own_chunk, *stats, *dq),
        [kv] + dq_shapes,
        [pltpu.VMEM((CHIP, 8 * CHIP), BF16)] * 2
        + [pltpu.VMEM((CHIP, CHIP), F32), pltpu.VMEM((CHIP, CHIP), BF16)],
        3 << 30, interpret,
    )


def per_device(count, interpret, queries, key_heads, value_heads, out_grad, segment, sink_logits):
    index = lax.axis_index(AXES)
    core, chip = index % 2, index // 2
    first = core == 0

    def sent(block, route):
        return lax.ppermute(block, AXES, route)

    def shifted(block, chips):
        return sent(block, [(i, (i + 2 * chips) % count) for i in range(count)])

    def crossed(block, bit):
        return lax.ppermute(block, AXES, [(i, i ^ bit) for i in range(count)])

    def in_row(i, hop):
        return i // 8 * 8 + (i // 2 + hop) % ROW * 2 + i % 2

    place = jnp.stack([core, chip]).astype(jnp.int32)
    def either(array, middle):
        return array[:, :middle], array[:, middle:]

    k_low, k_high = either(key_heads, HALF_KV)
    v_low, v_high = either(value_heads, HALF_KV)
    kv_low = jnp.concatenate([k_low, v_low], 1)
    kv_high = jnp.concatenate([k_high, v_high], 1)
    own, send = jnp.where(first, kv_low, kv_high), jnp.where(first, kv_high, kv_low)
    marks = jnp.pad(segment.astype(BF16)[None, :], ((0, 15), (0, 2 * HALF_KV - TOK)))
    kv_send = jnp.concatenate([send, marks], 0)
    queries, out_grad, kv_send = lax.optimization_barrier((queries, out_grad, kv_send))
    q_low, q_high = either(queries, 1024)
    g_low, g_high = either(out_grad, 1024)
    tokens_send = jnp.concatenate(
        [jnp.where(first, q_high, q_low), jnp.where(first, g_high, g_low)], 0
    )
    came, tokens_send = lax.optimization_barrier((crossed(kv_send, 1), tokens_send))
    marks_both = jnp.concatenate([marks[:, :TOK], came[TOK:, :TOK], marks[:, CHIP:]], 1)
    chunk = jnp.concatenate([own, came[:TOK], marks_both], 0)
    chunks = {0: chunk, HOPS: shifted(chunk, HOPS)}
    both = crossed(tokens_send, 1)
    tokens = prepared(place, queries, out_grad, both, interpret)
    stats = stats_of(
        0, False, place, sink_logits, tokens, chunk, chunk, (), interpret
    )
    *stats, chunks[HOPS] = lax.optimization_barrier((*stats, chunks[HOPS]))
    for hop in range(1, HOPS):
        within = chip % ROW + hop < ROW
        chunks[hop] = sent(
            jnp.where(within, chunk, chunks[HOPS]), [(i, in_row(i, hop)) for i in range(count)]
        )
    for hop in (HOPS, 1, 2, 3):
        stats = stats_of(
            hop, hop == 3, place, sink_logits, tokens, chunks[hop], chunk, stats, interpret
        )
    *stats, sink_block = stats
    gathered = lax.all_gather(sink_block, AXES[1:])
    dq, came_back = (), {}
    for hop in range(HOPS, 0, -1):
        part, *dq = parts_of(hop, place, tokens, chunks[hop], chunk, stats, dq, interpret)
        came_back[hop] = shifted(part, -hop)
        if hop + 2 in came_back:
            dq[0], came_back[hop + 2] = lax.optimization_barrier((dq[0], came_back[hop + 2]))
    total, dq_own, dq_peer = parts_of(0, place, tokens, chunk, chunk, stats, dq, interpret)

    def joined(mine, theirs):
        return jnp.where(
            first, jnp.concatenate([mine, theirs], 1), jnp.concatenate([theirs, mine], 1)
        )

    gathered, dq_peer = lax.optimization_barrier((gathered, dq_peer))

    def four_sums(value, low, high):
        near = value + crossed(value, low)
        return near + (crossed(value, high) + crossed(value, low | high))

    sink_grad = folded(gathered, interpret)
    if count > 16:
        sink_grad = four_sums(sink_grad, 8, 16)
    dq_came = crossed(dq_peer, 1)
    for part in came_back.values():
        total = total + part.astype(F32)
    total = total.astype(BF16)
    came, dq_came, sink_grad = lax.optimization_barrier(
        (crossed(total[TOK:], 1), dq_came, sink_grad)
    )
    if count > 16:
        sink_grad = four_sums(sink_grad, 64, 128)
        sink_grad = sink_grad + crossed(sink_grad, 32)
    else:
        sink_grad = sink_grad + crossed(sink_grad, 8)
    query_grad = joined(dq_own, dq_came)
    key_grad = joined(total[:TOK, :HALF_KV], came[:, :HALF_KV])
    value_grad = joined(total[:TOK, HALF_KV:], came[:, HALF_KV:])
    return query_grad, key_grad, value_grad, sink_grad


def solution(mesh, interpret=False):
    finer = Mesh(mesh.devices.reshape(-1, ROW, 2), AXES)
    rows = P(AXES, None)
    return jax.shard_map(
        functools.partial(per_device, mesh.size, interpret),
        mesh=finer,
        in_specs=(rows, rows, rows, rows, P(AXES), P()),
        out_specs=(rows, rows, rows, P()),
        check_vma=False,
    )
```

```python
import functools
import math

import jax
import jax.numpy as jnp
from jax import lax
from jax.experimental import pallas as pl
from jax.experimental.pallas import tpu as pltpu
from jax.sharding import PartitionSpec as P

KV_HEADS = 8
HEAD_DIM = 64
WINDOW = 1024
TOK = 128
CHIP = 2 * TOK
HOPS = WINDOW // CHIP
ROW = 4
SPAN = WINDOW + CHIP
HALF_KV = KV_HEADS // 2 * HEAD_DIM
SCALE = 1.0 / math.sqrt(HEAD_DIM)
EXP2_SCALE = SCALE * math.log2(math.e)
MASKED = -1e30
F32 = jnp.float32
BF16 = jnp.bfloat16


NT, NN = ((1,), (1,)), ((1,), (0,))


def dot(a, b, dims):
    return lax.dot_general(a, b, (dims, ((), ())), preferred_element_type=F32)


def mask_bias(place, chunk, own_chunk, hop):
    core, chip = place[0], place[1]
    key_seg = chunk[CHIP : CHIP + 16, :CHIP].astype(F32)[0:1]
    query_seg = own_chunk[CHIP : CHIP + 16, :CHIP].astype(F32)[0:1]
    key_seg = jnp.where(chip >= hop, key_seg, -1.0)
    column = jnp.transpose(jnp.broadcast_to(key_seg, (TOK, CHIP)))
    allowed = jnp.concatenate([column, column], 1) == query_seg
    if hop in (0, HOPS):
        query_pos = lax.broadcasted_iota(jnp.int32, (CHIP, CHIP), 1) ^ (core * TOK)
        key_pos = lax.broadcasted_iota(jnp.int32, (CHIP, CHIP), 0) ^ (core * TOK)
        inside = key_pos <= query_pos if hop == 0 else key_pos > query_pos
        allowed = allowed & inside
    return jnp.where(allowed, 0.0, MASKED)


def prep_kernel(place, q_own, g_own, both_peer, rows_all):
    query_all, grad_all = split_rows(rows_all)
    core = place[0]
    q_peer, g_peer = both_peer.at[:TOK, :], both_peer.at[TOK:, :]
    lane_half = lax.broadcasted_iota(jnp.int32, (CHIP, 128), 1) // HEAD_DIM
    for own, peer, out in ((q_own, q_peer, query_all), (g_own, g_peer, grad_all)):
        for pair in range(8):
            at = pl.ds(pl.multiple_of(core * 1024 + pair * 128, 128), 128)
            theirs = peer[:, pair * 128 : (pair + 1) * 128]
            rows = jnp.concatenate([own[:, at], theirs], 0).astype(F32)
            turned = pltpu.roll(rows, HEAD_DIM, 1)
            half = pair // 2 % 2
            for e in range(2):
                chosen = jnp.where(lane_half == half, rows if half == e else turned, 0.0)
                out[head_rows(2 * pair + e), :] = chosen.astype(BF16)


def split_rows(rows_all):
    return rows_all.at[: 16 * CHIP, :], rows_all.at[16 * CHIP :, :]


def head_rows(head):
    return slice(head * CHIP, (head + 1) * CHIP)


def lane_tile(tile, first_lane=0):
    return slice(first_lane + tile * 128, first_lane + tile * 128 + 128)


def stats_kernel(hop, last, place, sinks, rows_all, chunk, own_chunk, *refs):
    query_all, grad_all = split_rows(rows_all)
    before, after = refs[:3], refs[3:]
    if hop == 0:
        before, after = None, refs
    top_out, second, third = after[:3]
    bias, sink_rows = after[-2:]
    core = place[0]
    bias[...] = mask_bias(place, chunk, own_chunk, hop)
    for head in range(16):
        tile, at = head // 8, slice(head, head + 1)
        sink = sinks[core * 16 + head] * (1.0 / SCALE)
        s = dot(chunk[0:CHIP, lane_tile(tile)], query_all[head_rows(head), :], NT) + bias[...]
        dp = dot(chunk[0:CHIP, lane_tile(tile, HALF_KV)], grad_all[head_rows(head), :], NT)
        old = jnp.full((1, CHIP), sink, F32) if hop == 0 else before[0][at, :]
        top = jnp.maximum(old, jnp.max(s, 0, keepdims=True))
        ex = jnp.exp2((s - top) * EXP2_SCALE)
        fade = jnp.exp2((old - top) * EXP2_SCALE)
        denom = jnp.sum(ex, 0, keepdims=True)
        weighed = jnp.sum(ex * dp, 0, keepdims=True)
        if hop == 0:
            denom = denom + fade
        else:
            denom = denom + before[1][at, :] * fade
            weighed = weighed + before[2][at, :] * fade
        top_out[at, :] = top
        if last:
            share = 1.0 / denom
            delta = weighed * share
            second[at, :] = share
            third[at, :] = delta
            sink_rows[at, :] = -jnp.exp2((sink - top) * EXP2_SCALE) * share * delta
        else:
            second[at, :] = denom
            third[at, :] = weighed
    if last:
        sums = jnp.sum(sink_rows[...], 1, keepdims=True)
        after[3][...] = jnp.transpose(jnp.broadcast_to(sums, (16, 128)))[0:1, :]


def parts_kernel(
    hop, place, rows_all, chunk, own_chunk, tops, shares, deltas, *refs
):
    query_all, grad_all = split_rows(rows_all)
    weight, dscore, bias = refs[-3:]
    dq_in = None if hop == HOPS else refs[0]
    outs = refs[:-3] if hop == HOPS else refs[1:-3]
    kv_out = outs[0]
    bias[...] = mask_bias(place, chunk, own_chunk, hop)
    keys_t = jnp.transpose(chunk[0:CHIP, 0:CHIP].astype(F32)).astype(BF16)
    for tile in range(2):
        for n in range(8):
            head, span = 8 * tile + n, head_rows(n)
            at = slice(head, head + 1)
            s = dot(chunk[0:CHIP, lane_tile(tile)], query_all[head_rows(head), :], NT)
            dp = dot(
                chunk[0:CHIP, lane_tile(tile, HALF_KV)], grad_all[head_rows(head), :], NT
            )
            prob = jnp.exp2((s + bias[...] - tops[at, :]) * EXP2_SCALE) * shares[at, :]
            weight[tile, :, span] = prob.astype(BF16)
            dscore[tile, :, span] = (prob * (dp - deltas[at, :])).astype(BF16)
        rows = slice(8 * tile * CHIP, 8 * (tile + 1) * CHIP)
        value_part = dot(weight[tile], grad_all[rows, :], NN)
        key_part = dot(dscore[tile], query_all[rows, :], NN) * SCALE
        kv_out[:, lane_tile(tile)] = key_part.astype(kv_out.dtype)
        kv_out[:, lane_tile(tile, HALF_KV)] = value_part.astype(kv_out.dtype)
        for group in range(2):
            g = 2 * tile + group
            rows = slice(g * HEAD_DIM, (g + 1) * HEAD_DIM)
            dq_t = dot(
                keys_t[rows, :], dscore[tile, :, group * 1024 : (group + 1) * 1024], NN
            )
            if dq_in is not None:
                dq_t = dq_t + dq_in[rows, :]
            if hop > 0:
                outs[1][rows, :] = dq_t
                continue
            for pair in range(2):
                two = jnp.concatenate(
                    [dq_t[:, head_rows(2 * pair)], dq_t[:, head_rows(2 * pair + 1)]], 0
                )
                dq = (jnp.transpose(two) * SCALE).astype(BF16)
                outs[1][:, lane_tile(2 * g + pair)] = dq[:TOK]
                outs[2][:, lane_tile(2 * g + pair)] = dq[TOK:]


SMEM = pl.BlockSpec(memory_space=pltpu.SMEM)
VMEM = pl.BlockSpec(memory_space=pltpu.VMEM)
STAT = jax.ShapeDtypeStruct((16, CHIP), F32)


def run(kernel, name, n_scalars, operands, out_shape, scratch, flops, interpret):
    n_arrays = len(operands) - n_scalars
    return pl.pallas_call(
        kernel,
        name=name,
        in_specs=[SMEM] * n_scalars + [VMEM] * n_arrays,
        out_specs=[VMEM] * len(out_shape),
        out_shape=out_shape,
        scratch_shapes=scratch,
        compiler_params=pltpu.CompilerParams(vmem_limit_bytes=16 << 20),
        cost_estimate=pl.CostEstimate(flops=flops, transcendentals=0, bytes_accessed=1 << 20),
        interpret=interpret,
    )(*operands)


def prepared(place, queries, out_grad, both_peer, interpret):
    rows = jax.ShapeDtypeStruct((32 * CHIP, 128), BF16)
    return run(
        prep_kernel, "prep", 1, (place, queries, out_grad, both_peer),
        [rows], [], 1 << 30, interpret,
    )


def stats_of(hop, last, place, sinks, tokens, chunk, own_chunk, before, interpret):
    return run(
        functools.partial(stats_kernel, hop, last), f"stats_{hop}", 2,
        (place, sinks, *tokens, chunk, own_chunk, *before),
        [STAT] * 3 + [jax.ShapeDtypeStruct((1, 16), F32)] * last,
        [pltpu.VMEM((CHIP, CHIP), F32), pltpu.VMEM((16, CHIP), F32)], 2 << 30, interpret,
    )


def parts_of(hop, place, tokens, chunk, own_chunk, stats, dq, interpret):
    kv = jax.ShapeDtypeStruct((CHIP, 2 * HALF_KV), BF16 if hop else F32)
    if hop:
        dq_shapes = [jax.ShapeDtypeStruct((CHIP, 1024), F32)]
    else:
        dq_shapes = [jax.ShapeDtypeStruct((TOK, 1024), BF16)] * 2
    return run(
        functools.partial(parts_kernel, hop), f"parts_{hop}", 1,
        (place, *tokens, chunk, own_chunk, *stats, *dq),
        [kv] + dq_shapes,
        [pltpu.VMEM((2, CHIP, 8 * CHIP), BF16)] * 2 + [pltpu.VMEM((CHIP, CHIP), F32)],
        3 << 30, interpret,
    )


def per_device(count, interpret, queries, key_heads, value_heads, out_grad, segment, sink_logits):
    index = lax.axis_index("ctx")
    core, chip = index % 2, index // 2
    first = core == 0

    def sent(block, route):
        return lax.ppermute(block, "ctx", route)

    def shifted(block, chips):
        return sent(block, [(i, (i + 2 * chips) % count) for i in range(count)])

    def crossed(block, bit):
        return lax.ppermute(block, "ctx", [(i, i ^ bit) for i in range(count)])

    def in_row(i, hop):
        return i // 8 * 8 + (i // 2 + hop) % ROW * 2 + i % 2

    place = jnp.stack([core, chip]).astype(jnp.int32)
    def either(array, middle):
        return array[:, :middle], array[:, middle:]

    k_low, k_high = either(key_heads, HALF_KV)
    v_low, v_high = either(value_heads, HALF_KV)
    kv_low = jnp.concatenate([k_low, v_low], 1)
    kv_high = jnp.concatenate([k_high, v_high], 1)
    own, send = jnp.where(first, kv_low, kv_high), jnp.where(first, kv_high, kv_low)
    marks = jnp.pad(segment.astype(BF16)[None, :], ((0, 15), (0, 2 * HALF_KV - TOK)))
    kv_send = jnp.concatenate([send, marks], 0)
    queries, out_grad, kv_send = lax.optimization_barrier((queries, out_grad, kv_send))
    q_low, q_high = either(queries, 1024)
    g_low, g_high = either(out_grad, 1024)
    tokens_send = jnp.concatenate(
        [jnp.where(first, q_high, q_low), jnp.where(first, g_high, g_low)], 0
    )
    came, tokens_send = lax.optimization_barrier((crossed(kv_send, 1), tokens_send))
    marks_both = jnp.concatenate([marks[:, :TOK], came[TOK:, :TOK], marks[:, CHIP:]], 1)
    chunk = jnp.concatenate([own, came[:TOK], marks_both], 0)
    chunks = {0: chunk, HOPS: shifted(chunk, HOPS)}
    both = crossed(tokens_send, 1)
    tokens = prepared(place, queries, out_grad, both, interpret)
    stats = stats_of(
        0, False, place, sink_logits, tokens, chunk, chunk, (), interpret
    )
    *stats, chunks[HOPS] = lax.optimization_barrier((*stats, chunks[HOPS]))
    for hop in range(1, HOPS):
        within = chip % ROW + hop < ROW
        chunks[hop] = sent(
            jnp.where(within, chunk, chunks[HOPS]), [(i, in_row(i, hop)) for i in range(count)]
        )
    for hop in (HOPS, 1, 2, 3):
        stats = stats_of(
            hop, hop == 3, place, sink_logits, tokens, chunks[hop], chunk, stats, interpret
        )
    *stats, sink_row = stats
    sink_grad = sink_row.reshape(16)
    bits = [bit for bit in (4, 16, 32, 128, 8, 64, 2) if bit < count]

    def widened(value):
        return value + crossed(value, bits.pop(0)) if bits else value

    dq, came_back = (), {}
    for hop in range(HOPS, 0, -1):
        part, *dq = parts_of(hop, place, tokens, chunks[hop], chunk, stats, dq, interpret)
        came_back[hop] = shifted(part, -hop)
        sink_grad = widened(sink_grad)
        if hop < HOPS:
            dq[0], sink_grad, came_back[hop + 1] = lax.optimization_barrier(
                (dq[0], sink_grad, came_back[hop + 1])
            )
        else:
            dq[0], sink_grad = lax.optimization_barrier((dq[0], sink_grad))
    total, dq_own, dq_peer = parts_of(0, place, tokens, chunk, chunk, stats, dq, interpret)
    dq_own, dq_peer, sink_grad = lax.optimization_barrier(
        (dq_own, dq_peer, widened(sink_grad))
    )

    def joined(mine, theirs):
        return jnp.where(
            first, jnp.concatenate([mine, theirs], 1), jnp.concatenate([theirs, mine], 1)
        )

    query_grad = joined(dq_own, crossed(dq_peer, 1))
    for part in came_back.values():
        total = total + part.astype(F32)
    total, query_grad, sink_grad = lax.optimization_barrier(
        (total.astype(BF16), query_grad, widened(sink_grad))
    )
    came = crossed(total[TOK:], 1)
    key_grad = joined(total[:TOK, :HALF_KV], came[:, :HALF_KV])
    value_grad = joined(total[:TOK, HALF_KV:], came[:, HALF_KV:])
    key_grad, value_grad, sink_grad = lax.optimization_barrier(
        (key_grad, value_grad, widened(sink_grad))
    )
    other = crossed(sink_grad, 1)
    sink_grad = jnp.where(
        first, jnp.concatenate([sink_grad, other]), jnp.concatenate([other, sink_grad])
    )
    return query_grad, key_grad, value_grad, sink_grad


def solution(mesh, interpret=False):
    rows = P("ctx", None)
    return jax.shard_map(
        functools.partial(per_device, mesh.size, interpret),
        mesh=mesh,
        in_specs=(rows, rows, rows, rows, P("ctx"), P()),
        out_specs=(rows, rows, rows, P()),
        check_vma=False,
    )
```

```python
import functools
import math

import jax
import jax.numpy as jnp
from jax import lax
from jax.experimental import pallas as pl
from jax.experimental.pallas import tpu as pltpu
from jax.sharding import PartitionSpec as P

KV_HEADS = 8
HEAD_DIM = 64
WINDOW = 1024
TOK = 128
CHIP = 2 * TOK
HOPS = WINDOW // CHIP
ROW = 4
SPAN = WINDOW + CHIP
HALF_KV = KV_HEADS // 2 * HEAD_DIM
SCALE = 1.0 / math.sqrt(HEAD_DIM)
EXP2_SCALE = SCALE * math.log2(math.e)
MASKED = -1e30
F32 = jnp.float32
BF16 = jnp.bfloat16


NT, NN = ((1,), (1,)), ((1,), (0,))


def dot(a, b, dims):
    return lax.dot_general(a, b, (dims, ((), ())), preferred_element_type=F32)


def mask_bias(place, chunk, own_chunk, hop):
    core, chip = place[0], place[1]
    key_seg = chunk[CHIP : CHIP + 16, :CHIP].astype(F32)[0:1]
    query_seg = own_chunk[CHIP : CHIP + 16, :CHIP].astype(F32)[0:1]
    key_seg = jnp.where(chip >= hop, key_seg, -1.0)
    column = jnp.transpose(jnp.broadcast_to(key_seg, (TOK, CHIP)))
    allowed = jnp.concatenate([column, column], 1) == query_seg
    if hop in (0, HOPS):
        query_pos = lax.broadcasted_iota(jnp.int32, (CHIP, CHIP), 1) ^ (core * TOK)
        key_pos = lax.broadcasted_iota(jnp.int32, (CHIP, CHIP), 0) ^ (core * TOK)
        inside = key_pos <= query_pos if hop == 0 else key_pos > query_pos
        allowed = allowed & inside
    return jnp.where(allowed, 0.0, MASKED)


def prep_kernel(place, q_own, g_own, both_peer, rows_all):
    query_all, grad_all = split_rows(rows_all)
    core = place[0]
    q_peer, g_peer = both_peer.at[:TOK, :], both_peer.at[TOK:, :]
    lane_half = lax.broadcasted_iota(jnp.int32, (CHIP, 128), 1) // HEAD_DIM
    for own, peer, out in ((q_own, q_peer, query_all), (g_own, g_peer, grad_all)):
        for pair in range(8):
            at = pl.ds(pl.multiple_of(core * 1024 + pair * 128, 128), 128)
            theirs = peer[:, pair * 128 : (pair + 1) * 128]
            rows = jnp.concatenate([own[:, at], theirs], 0).astype(F32)
            turned = pltpu.roll(rows, HEAD_DIM, 1)
            half = pair // 2 % 2
            for e in range(2):
                chosen = jnp.where(lane_half == half, rows if half == e else turned, 0.0)
                out[head_rows(2 * pair + e), :] = chosen.astype(BF16)


def split_rows(rows_all):
    return rows_all.at[: 16 * CHIP, :], rows_all.at[16 * CHIP :, :]


def head_rows(head):
    return slice(head * CHIP, (head + 1) * CHIP)


def lane_tile(tile, first_lane=0):
    return slice(first_lane + tile * 128, first_lane + tile * 128 + 128)


def stats_kernel(hop, last, place, sinks, rows_all, chunk, own_chunk, *refs):
    query_all, grad_all = split_rows(rows_all)
    before, after = refs[:3], refs[3:]
    if hop == 0:
        before, after = None, refs
    top_out, second, third = after[:3]
    bias, sink_rows = after[-2:]
    core = place[0]
    bias[...] = mask_bias(place, chunk, own_chunk, hop)
    for head in range(16):
        tile, at = head // 8, slice(head, head + 1)
        sink = sinks[core * 16 + head] * (1.0 / SCALE)
        s = dot(chunk[0:CHIP, lane_tile(tile)], query_all[head_rows(head), :], NT) + bias[...]
        dp = dot(chunk[0:CHIP, lane_tile(tile, HALF_KV)], grad_all[head_rows(head), :], NT)
        old = jnp.full((1, CHIP), sink, F32) if hop == 0 else before[0][at, :]
        top = jnp.maximum(old, jnp.max(s, 0, keepdims=True))
        ex = jnp.exp2((s - top) * EXP2_SCALE)
        fade = jnp.exp2((old - top) * EXP2_SCALE)
        denom = jnp.sum(ex, 0, keepdims=True)
        weighed = jnp.sum(ex * dp, 0, keepdims=True)
        if hop == 0:
            denom = denom + fade
        else:
            denom = denom + before[1][at, :] * fade
            weighed = weighed + before[2][at, :] * fade
        top_out[at, :] = top
        if last:
            share = 1.0 / denom
            delta = weighed * share
            second[at, :] = share
            third[at, :] = delta
            sink_rows[at, :] = -jnp.exp2((sink - top) * EXP2_SCALE) * share * delta
        else:
            second[at, :] = denom
            third[at, :] = weighed
    if last:
        sums = jnp.sum(sink_rows[...], 1, keepdims=True)
        after[3][...] = jnp.transpose(jnp.broadcast_to(sums, (16, 128)))[0:1, :]


def parts_kernel(
    hop, place, rows_all, chunk, own_chunk, tops, shares, deltas, *refs
):
    query_all, grad_all = split_rows(rows_all)
    weight, dscore, bias = refs[-3:]
    dq_in = None if hop == HOPS else refs[0]
    outs = refs[:-3] if hop == HOPS else refs[1:-3]
    kv_out = outs[0]
    bias[...] = mask_bias(place, chunk, own_chunk, hop)
    keys_t = jnp.transpose(chunk[0:CHIP, 0:CHIP].astype(F32)).astype(BF16)
    for tile in range(2):
        for n in range(8):
            head, span = 8 * tile + n, head_rows(n)
            at = slice(head, head + 1)
            s = dot(chunk[0:CHIP, lane_tile(tile)], query_all[head_rows(head), :], NT)
            dp = dot(
                chunk[0:CHIP, lane_tile(tile, HALF_KV)], grad_all[head_rows(head), :], NT
            )
            prob = jnp.exp2((s + bias[...] - tops[at, :]) * EXP2_SCALE) * shares[at, :]
            weight[tile, :, span] = prob.astype(BF16)
            dscore[tile, :, span] = (prob * (dp - deltas[at, :])).astype(BF16)
        rows = slice(8 * tile * CHIP, 8 * (tile + 1) * CHIP)
        value_part = dot(weight[tile], grad_all[rows, :], NN)
        key_part = dot(dscore[tile], query_all[rows, :], NN) * SCALE
        kv_out[:, lane_tile(tile)] = key_part.astype(kv_out.dtype)
        kv_out[:, lane_tile(tile, HALF_KV)] = value_part.astype(kv_out.dtype)
        for group in range(2):
            g = 2 * tile + group
            rows = slice(g * HEAD_DIM, (g + 1) * HEAD_DIM)
            dq_t = dot(
                keys_t[rows, :], dscore[tile, :, group * 1024 : (group + 1) * 1024], NN
            )
            if dq_in is not None:
                dq_t = dq_t + dq_in[rows, :]
            if hop > 0:
                outs[1][rows, :] = dq_t
                continue
            for pair in range(2):
                two = jnp.concatenate(
                    [dq_t[:, head_rows(2 * pair)], dq_t[:, head_rows(2 * pair + 1)]], 0
                )
                dq = (jnp.transpose(two) * SCALE).astype(BF16)
                outs[1][:, lane_tile(2 * g + pair)] = dq[:TOK]
                outs[2][:, lane_tile(2 * g + pair)] = dq[TOK:]


SMEM = pl.BlockSpec(memory_space=pltpu.SMEM)
VMEM = pl.BlockSpec(memory_space=pltpu.VMEM)
STAT = jax.ShapeDtypeStruct((16, CHIP), F32)


def run(kernel, name, n_scalars, operands, out_shape, scratch, flops, interpret):
    n_arrays = len(operands) - n_scalars
    return pl.pallas_call(
        kernel,
        name=name,
        in_specs=[SMEM] * n_scalars + [VMEM] * n_arrays,
        out_specs=[VMEM] * len(out_shape),
        out_shape=out_shape,
        scratch_shapes=scratch,
        compiler_params=pltpu.CompilerParams(vmem_limit_bytes=16 << 20),
        cost_estimate=pl.CostEstimate(flops=flops, transcendentals=0, bytes_accessed=1 << 20),
        interpret=interpret,
    )(*operands)


def prepared(place, queries, out_grad, both_peer, interpret):
    rows = jax.ShapeDtypeStruct((32 * CHIP, 128), BF16)
    return run(
        prep_kernel, "prep", 1, (place, queries, out_grad, both_peer),
        [rows], [], 1 << 30, interpret,
    )


def stats_of(hop, last, place, sinks, tokens, chunk, own_chunk, before, interpret):
    return run(
        functools.partial(stats_kernel, hop, last), f"stats_{hop}", 2,
        (place, sinks, *tokens, chunk, own_chunk, *before),
        [STAT] * 3 + [jax.ShapeDtypeStruct((1, 16), F32)] * last,
        [pltpu.VMEM((CHIP, CHIP), F32), pltpu.VMEM((16, CHIP), F32)], 2 << 30, interpret,
    )


def parts_of(hop, place, tokens, chunk, own_chunk, stats, dq, interpret):
    kv = jax.ShapeDtypeStruct((CHIP, 2 * HALF_KV), BF16 if hop else F32)
    if hop:
        dq_shapes = [jax.ShapeDtypeStruct((CHIP, 1024), F32)]
    else:
        dq_shapes = [jax.ShapeDtypeStruct((TOK, 1024), BF16)] * 2
    return run(
        functools.partial(parts_kernel, hop), f"parts_{hop}", 1,
        (place, *tokens, chunk, own_chunk, *stats, *dq),
        [kv] + dq_shapes,
        [pltpu.VMEM((2, CHIP, 8 * CHIP), BF16)] * 2 + [pltpu.VMEM((CHIP, CHIP), F32)],
        3 << 30, interpret,
    )


def per_device(count, interpret, queries, key_heads, value_heads, out_grad, segment, sink_logits):
    index = lax.axis_index("ctx")
    core, chip = index % 2, index // 2
    first = core == 0

    def sent(block, route):
        return lax.ppermute(block, "ctx", route)

    def shifted(block, chips):
        return sent(block, [(i, (i + 2 * chips) % count) for i in range(count)])

    def crossed(block, bit):
        return lax.ppermute(block, "ctx", [(i, i ^ bit) for i in range(count)])

    def in_row(i, hop):
        return i // 8 * 8 + (i // 2 + hop) % ROW * 2 + i % 2

    place = jnp.stack([core, chip]).astype(jnp.int32)
    def either(array, middle):
        return array[:, :middle], array[:, middle:]

    k_low, k_high = either(key_heads, HALF_KV)
    v_low, v_high = either(value_heads, HALF_KV)
    kv_low = jnp.concatenate([k_low, v_low], 1)
    kv_high = jnp.concatenate([k_high, v_high], 1)
    own, send = jnp.where(first, kv_low, kv_high), jnp.where(first, kv_high, kv_low)
    marks = jnp.pad(segment.astype(BF16)[None, :], ((0, 15), (0, 2 * HALF_KV - TOK)))
    kv_send = jnp.concatenate([send, marks], 0)
    queries, out_grad, kv_send = lax.optimization_barrier((queries, out_grad, kv_send))
    q_low, q_high = either(queries, 1024)
    g_low, g_high = either(out_grad, 1024)
    tokens_send = jnp.concatenate(
        [jnp.where(first, q_high, q_low), jnp.where(first, g_high, g_low)], 0
    )
    came, tokens_send = lax.optimization_barrier((crossed(kv_send, 1), tokens_send))
    marks_both = jnp.concatenate([marks[:, :TOK], came[TOK:, :TOK], marks[:, CHIP:]], 1)
    chunk = jnp.concatenate([own, came[:TOK], marks_both], 0)
    chunks = {0: chunk, HOPS: shifted(chunk, HOPS)}
    both = crossed(tokens_send, 1)
    tokens = prepared(place, queries, out_grad, both, interpret)
    stats = stats_of(
        0, False, place, sink_logits, tokens, chunk, chunk, (), interpret
    )
    *stats, chunks[HOPS] = lax.optimization_barrier((*stats, chunks[HOPS]))
    def row_place(i):
        return i // 2 % ROW

    for hop in (1, 3):
        within = chip % ROW + hop < ROW
        chunks[hop] = sent(
            jnp.where(within, chunk, chunks[HOPS]), [(i, in_row(i, hop)) for i in range(count)]
        )
    crossing = [(i, in_row(i, 2)) for i in range(count) if row_place(i) == 2]
    relayed = [(i, in_row(i, 1)) for i in range(count) if row_place(i) < ROW - 1]
    chunks[2] = sent(chunks[HOPS], crossing) + sent(chunks[1], relayed)
    for hop in (HOPS, 1, 3, 2):
        stats = stats_of(
            hop, hop == 2, place, sink_logits, tokens, chunks[hop], chunk, stats, interpret
        )
    *stats, sink_row = stats
    sink_grad = sink_row.reshape(16)
    bits = [bit for bit in (4, 16, 32, 128, 8, 64, 2) if bit < count]

    def widened(value):
        return value + crossed(value, bits.pop(0)) if bits else value

    dq, came_back = (), {}
    for hop in range(HOPS, 0, -1):
        part, *dq = parts_of(hop, place, tokens, chunks[hop], chunk, stats, dq, interpret)
        came_back[hop] = shifted(part, -hop)
        sink_grad = widened(sink_grad)
        if hop < HOPS:
            dq[0], sink_grad, came_back[hop + 1] = lax.optimization_barrier(
                (dq[0], sink_grad, came_back[hop + 1])
            )
        else:
            dq[0], sink_grad = lax.optimization_barrier((dq[0], sink_grad))
    total, dq_own, dq_peer = parts_of(0, place, tokens, chunk, chunk, stats, dq, interpret)
    dq_own, dq_peer, sink_grad = lax.optimization_barrier(
        (dq_own, dq_peer, widened(sink_grad))
    )

    def joined(mine, theirs):
        return jnp.where(
            first, jnp.concatenate([mine, theirs], 1), jnp.concatenate([theirs, mine], 1)
        )

    query_grad = joined(dq_own, crossed(dq_peer, 1))
    for part in came_back.values():
        total = total + part.astype(F32)
    total, sink_grad = lax.optimization_barrier((total.astype(BF16), widened(sink_grad)))
    came, query_grad, sink_grad = lax.optimization_barrier(
        (crossed(total[TOK:], 1), query_grad, widened(sink_grad))
    )
    key_grad = joined(total[:TOK, :HALF_KV], came[:, :HALF_KV])
    value_grad = joined(total[:TOK, HALF_KV:], came[:, HALF_KV:])
    other = crossed(sink_grad, 1)
    sink_grad = jnp.where(
        first, jnp.concatenate([sink_grad, other]), jnp.concatenate([other, sink_grad])
    )
    return query_grad, key_grad, value_grad, sink_grad


def solution(mesh, interpret=False):
    rows = P("ctx", None)
    return jax.shard_map(
        functools.partial(per_device, mesh.size, interpret),
        mesh=mesh,
        in_specs=(rows, rows, rows, rows, P("ctx"), P()),
        out_specs=(rows, rows, rows, P()),
        check_vma=False,
    )
```

```python
import functools
import math

import jax
import jax.numpy as jnp
from jax import lax
from jax.experimental import pallas as pl
from jax.experimental.pallas import tpu as pltpu
from jax.sharding import PartitionSpec as P

KV_HEADS = 8
HEAD_DIM = 64
WINDOW = 1024
TOK = 128
CHIP = 2 * TOK
HOPS = WINDOW // CHIP
ROW = 4
SPAN = WINDOW + CHIP
HALF_KV = KV_HEADS // 2 * HEAD_DIM
SCALE = 1.0 / math.sqrt(HEAD_DIM)
EXP2_SCALE = SCALE * math.log2(math.e)
MASKED = -1e30
F32 = jnp.float32
BF16 = jnp.bfloat16


NT, NN = ((1,), (1,)), ((1,), (0,))


def dot(a, b, dims):
    return lax.dot_general(a, b, (dims, ((), ())), preferred_element_type=F32)


def mask_bias(place, chunk, own_chunk, hop):
    core, chip = place[0], place[1]
    key_seg = chunk[CHIP : CHIP + 16, :CHIP].astype(F32)[0:1]
    query_seg = own_chunk[CHIP : CHIP + 16, :CHIP].astype(F32)[0:1]
    key_seg = jnp.where(chip >= hop, key_seg, -1.0)
    column = jnp.transpose(jnp.broadcast_to(key_seg, (TOK, CHIP)))
    allowed = jnp.concatenate([column, column], 1) == query_seg
    if hop in (0, HOPS):
        query_pos = lax.broadcasted_iota(jnp.int32, (CHIP, CHIP), 1) ^ (core * TOK)
        key_pos = lax.broadcasted_iota(jnp.int32, (CHIP, CHIP), 0) ^ (core * TOK)
        inside = key_pos <= query_pos if hop == 0 else key_pos > query_pos
        allowed = allowed & inside
    return jnp.where(allowed, 0.0, MASKED)


def prep_kernel(place, q_own, g_own, both_peer, rows_all):
    query_all, grad_all = split_rows(rows_all)
    core = place[0]
    q_peer, g_peer = both_peer.at[:TOK, :], both_peer.at[TOK:, :]
    lane_half = lax.broadcasted_iota(jnp.int32, (CHIP, 128), 1) // HEAD_DIM
    for own, peer, out in ((q_own, q_peer, query_all), (g_own, g_peer, grad_all)):
        for pair in range(8):
            at = pl.ds(pl.multiple_of(core * 1024 + pair * 128, 128), 128)
            theirs = peer[:, pair * 128 : (pair + 1) * 128]
            rows = jnp.concatenate([own[:, at], theirs], 0).astype(F32)
            turned = pltpu.roll(rows, HEAD_DIM, 1)
            half = pair // 2 % 2
            for e in range(2):
                chosen = jnp.where(lane_half == half, rows if half == e else turned, 0.0)
                out[head_rows(2 * pair + e), :] = chosen.astype(BF16)


def split_rows(rows_all):
    return rows_all.at[: 16 * CHIP, :], rows_all.at[16 * CHIP :, :]


def head_rows(head):
    return slice(head * CHIP, (head + 1) * CHIP)


def lane_tile(tile, first_lane=0):
    return slice(first_lane + tile * 128, first_lane + tile * 128 + 128)


def stats_kernel(hop, last, place, sinks, rows_all, chunk, own_chunk, *refs):
    query_all, grad_all = split_rows(rows_all)
    before, after = refs[:3], refs[3:]
    if hop == 0:
        before, after = None, refs
    top_out, second, third = after[:3]
    bias, sink_rows = after[-2:]
    core = place[0]
    bias[...] = mask_bias(place, chunk, own_chunk, hop)
    for head in range(16):
        tile, at = head // 8, slice(head, head + 1)
        sink = sinks[core * 16 + head] * (1.0 / SCALE)
        s = dot(chunk[0:CHIP, lane_tile(tile)], query_all[head_rows(head), :], NT) + bias[...]
        dp = dot(chunk[0:CHIP, lane_tile(tile, HALF_KV)], grad_all[head_rows(head), :], NT)
        old = jnp.full((1, CHIP), sink, F32) if hop == 0 else before[0][at, :]
        top = jnp.maximum(old, jnp.max(s, 0, keepdims=True))
        ex = jnp.exp2((s - top) * EXP2_SCALE)
        fade = jnp.exp2((old - top) * EXP2_SCALE)
        denom = jnp.sum(ex, 0, keepdims=True)
        weighed = jnp.sum(ex * dp, 0, keepdims=True)
        if hop == 0:
            denom = denom + fade
        else:
            denom = denom + before[1][at, :] * fade
            weighed = weighed + before[2][at, :] * fade
        top_out[at, :] = top
        if last:
            share = 1.0 / denom
            delta = weighed * share
            second[at, :] = share
            third[at, :] = delta
            sink_rows[at, :] = -jnp.exp2((sink - top) * EXP2_SCALE) * share * delta
        else:
            second[at, :] = denom
            third[at, :] = weighed
    if last:
        sums = jnp.sum(sink_rows[...], 1, keepdims=True)
        after[3][...] = jnp.transpose(jnp.broadcast_to(sums, (16, 128)))[0:1, :]


def parts_kernel(
    hop, place, rows_all, chunk, own_chunk, tops, shares, deltas, *refs
):
    query_all, grad_all = split_rows(rows_all)
    weight, dscore, bias = refs[-3:]
    dq_in = None if hop == HOPS else refs[0]
    outs = refs[:-3] if hop == HOPS else refs[1:-3]
    kv_out = outs[0]
    bias[...] = mask_bias(place, chunk, own_chunk, hop)
    keys_t = jnp.transpose(chunk[0:CHIP, 0:CHIP].astype(F32)).astype(BF16)
    for tile in range(2):
        for n in range(8):
            head, span = 8 * tile + n, head_rows(n)
            at = slice(head, head + 1)
            s = dot(chunk[0:CHIP, lane_tile(tile)], query_all[head_rows(head), :], NT)
            dp = dot(
                chunk[0:CHIP, lane_tile(tile, HALF_KV)], grad_all[head_rows(head), :], NT
            )
            prob = jnp.exp2((s + bias[...] - tops[at, :]) * EXP2_SCALE) * shares[at, :]
            weight[tile, :, span] = prob.astype(BF16)
            dscore[tile, :, span] = (prob * (dp - deltas[at, :])).astype(BF16)
        rows = slice(8 * tile * CHIP, 8 * (tile + 1) * CHIP)
        value_part = dot(weight[tile], grad_all[rows, :], NN)
        key_part = dot(dscore[tile], query_all[rows, :], NN) * SCALE
        kv_out[:, lane_tile(tile)] = key_part.astype(kv_out.dtype)
        kv_out[:, lane_tile(tile, HALF_KV)] = value_part.astype(kv_out.dtype)
        for group in range(2):
            g = 2 * tile + group
            rows = slice(g * HEAD_DIM, (g + 1) * HEAD_DIM)
            dq_t = dot(
                keys_t[rows, :], dscore[tile, :, group * 1024 : (group + 1) * 1024], NN
            )
            if dq_in is not None:
                dq_t = dq_t + dq_in[rows, :]
            if hop > 0:
                outs[1][rows, :] = dq_t
                continue
            for pair in range(2):
                two = jnp.concatenate(
                    [dq_t[:, head_rows(2 * pair)], dq_t[:, head_rows(2 * pair + 1)]], 0
                )
                dq = (jnp.transpose(two) * SCALE).astype(BF16)
                outs[1][:, lane_tile(2 * g + pair)] = dq[:TOK]
                outs[2][:, lane_tile(2 * g + pair)] = dq[TOK:]


SMEM = pl.BlockSpec(memory_space=pltpu.SMEM)
VMEM = pl.BlockSpec(memory_space=pltpu.VMEM)
STAT = jax.ShapeDtypeStruct((16, CHIP), F32)


def run(kernel, name, n_scalars, operands, out_shape, scratch, flops, interpret):
    n_arrays = len(operands) - n_scalars
    return pl.pallas_call(
        kernel,
        name=name,
        in_specs=[SMEM] * n_scalars + [VMEM] * n_arrays,
        out_specs=[VMEM] * len(out_shape),
        out_shape=out_shape,
        scratch_shapes=scratch,
        compiler_params=pltpu.CompilerParams(vmem_limit_bytes=16 << 20),
        cost_estimate=pl.CostEstimate(flops=flops, transcendentals=0, bytes_accessed=1 << 20),
        interpret=interpret,
    )(*operands)


def prepared(place, queries, out_grad, both_peer, interpret):
    rows = jax.ShapeDtypeStruct((32 * CHIP, 128), BF16)
    return run(
        prep_kernel, "prep", 1, (place, queries, out_grad, both_peer),
        [rows], [], 1 << 30, interpret,
    )


def stats_of(hop, last, place, sinks, tokens, chunk, own_chunk, before, interpret):
    return run(
        functools.partial(stats_kernel, hop, last), f"stats_{hop}", 2,
        (place, sinks, *tokens, chunk, own_chunk, *before),
        [STAT] * 3 + [jax.ShapeDtypeStruct((1, 16), F32)] * last,
        [pltpu.VMEM((CHIP, CHIP), F32), pltpu.VMEM((16, CHIP), F32)], 2 << 30, interpret,
    )


def parts_of(hop, place, tokens, chunk, own_chunk, stats, dq, interpret):
    kv = jax.ShapeDtypeStruct((CHIP, 2 * HALF_KV), BF16 if hop else F32)
    if hop:
        dq_shapes = [jax.ShapeDtypeStruct((CHIP, 1024), F32)]
    else:
        dq_shapes = [jax.ShapeDtypeStruct((TOK, 1024), BF16)] * 2
    return run(
        functools.partial(parts_kernel, hop), f"parts_{hop}", 1,
        (place, *tokens, chunk, own_chunk, *stats, *dq),
        [kv] + dq_shapes,
        [pltpu.VMEM((2, CHIP, 8 * CHIP), BF16)] * 2 + [pltpu.VMEM((CHIP, CHIP), F32)],
        3 << 30, interpret,
    )


def per_device(count, interpret, queries, key_heads, value_heads, out_grad, segment, sink_logits):
    index = lax.axis_index("ctx")
    core, chip = index % 2, index // 2
    first = core == 0

    def sent(block, route):
        return lax.ppermute(block, "ctx", route)

    def shifted(block, chips):
        return sent(block, [(i, (i + 2 * chips) % count) for i in range(count)])

    def crossed(block, bit):
        return lax.ppermute(block, "ctx", [(i, i ^ bit) for i in range(count)])

    def in_row(i, hop):
        return i // 8 * 8 + (i // 2 + hop) % ROW * 2 + i % 2

    place = jnp.stack([core, chip]).astype(jnp.int32)
    def either(array, middle):
        return array[:, :middle], array[:, middle:]

    k_low, k_high = either(key_heads, HALF_KV)
    v_low, v_high = either(value_heads, HALF_KV)
    kv_low = jnp.concatenate([k_low, v_low], 1)
    kv_high = jnp.concatenate([k_high, v_high], 1)
    own, send = jnp.where(first, kv_low, kv_high), jnp.where(first, kv_high, kv_low)
    marks = jnp.pad(segment.astype(BF16)[None, :], ((0, 15), (0, 2 * HALF_KV - TOK)))
    kv_send = jnp.concatenate([send, marks], 0)
    queries, out_grad, kv_send = lax.optimization_barrier((queries, out_grad, kv_send))
    q_low, q_high = either(queries, 1024)
    g_low, g_high = either(out_grad, 1024)
    tokens_send = jnp.concatenate(
        [jnp.where(first, q_high, q_low), jnp.where(first, g_high, g_low)], 0
    )
    came, tokens_send = lax.optimization_barrier((crossed(kv_send, 1), tokens_send))
    marks_both = jnp.concatenate([marks[:, :TOK], came[TOK:, :TOK], marks[:, CHIP:]], 1)
    chunk = jnp.concatenate([own, came[:TOK], marks_both], 0)
    chunks = {0: chunk, HOPS: shifted(chunk, HOPS)}
    both = crossed(tokens_send, 1)
    tokens = prepared(place, queries, out_grad, both, interpret)
    stats = stats_of(
        0, False, place, sink_logits, tokens, chunk, chunk, (), interpret
    )
    *stats, chunks[HOPS] = lax.optimization_barrier((*stats, chunks[HOPS]))
    for hop in range(1, HOPS):
        within = chip % ROW + hop < ROW
        chunks[hop] = sent(
            jnp.where(within, chunk, chunks[HOPS]), [(i, in_row(i, hop)) for i in range(count)]
        )
    for hop in (HOPS, 1, 3, 2):
        stats = stats_of(
            hop, hop == 2, place, sink_logits, tokens, chunks[hop], chunk, stats, interpret
        )
    *stats, sink_row = stats
    sink_grad = sink_row.reshape(16)
    bits = [bit for bit in (4, 16, 32, 128, 8, 64, 2) if bit < count]

    def widened(value):
        return value + crossed(value, bits.pop(0)) if bits else value

    dq, came_back = (), {}
    for hop in range(HOPS, 0, -1):
        part, *dq = parts_of(hop, place, tokens, chunks[hop], chunk, stats, dq, interpret)
        came_back[hop] = shifted(part, -hop)
        sink_grad = widened(sink_grad)
        if hop + 2 in came_back:
            dq[0], sink_grad, came_back[hop + 2] = lax.optimization_barrier(
                (dq[0], sink_grad, came_back[hop + 2])
            )
        else:
            dq[0], sink_grad = lax.optimization_barrier((dq[0], sink_grad))
    total, dq_own, dq_peer = parts_of(0, place, tokens, chunk, chunk, stats, dq, interpret)
    dq_own, dq_peer, sink_grad = lax.optimization_barrier(
        (dq_own, dq_peer, widened(sink_grad))
    )

    def joined(mine, theirs):
        return jnp.where(
            first, jnp.concatenate([mine, theirs], 1), jnp.concatenate([theirs, mine], 1)
        )

    query_grad = joined(dq_own, crossed(dq_peer, 1))
    for part in came_back.values():
        total = total + part.astype(F32)
    total, sink_grad = lax.optimization_barrier((total.astype(BF16), widened(sink_grad)))
    came, query_grad, sink_grad = lax.optimization_barrier(
        (crossed(total[TOK:], 1), query_grad, widened(sink_grad))
    )
    key_grad = joined(total[:TOK, :HALF_KV], came[:, :HALF_KV])
    value_grad = joined(total[:TOK, HALF_KV:], came[:, HALF_KV:])
    other = crossed(sink_grad, 1)
    sink_grad = jnp.where(
        first, jnp.concatenate([sink_grad, other]), jnp.concatenate([other, sink_grad])
    )
    return query_grad, key_grad, value_grad, sink_grad


def solution(mesh, interpret=False):
    rows = P("ctx", None)
    return jax.shard_map(
        functools.partial(per_device, mesh.size, interpret),
        mesh=mesh,
        in_specs=(rows, rows, rows, rows, P("ctx"), P()),
        out_specs=(rows, rows, rows, P()),
        check_vma=False,
    )
```
